512 devices in a mesh: layer: 4 (over x), feat: 32 (over z, y_lo), width: 4 (over y_hi, core).
Axes of the slice: x: 4, y: 8 (y_hi: 2, y_lo: 4; y = y_hi * 4 + y_lo), z: 8, core: 2. Of those that a mesh axis runs over, the one named last changes fastest.
Arguments:
- residuals: bfloat16 [4, 1024, 2304], P('layer', 'feat', 'width'), may hold values from -6 to 6
- cotangent: bfloat16 [4, 1024, 2304], P('layer', 'feat', 'width'), may hold values from -6 to 6
- enc_weight: bfloat16 [4, 2304, 8192], P('layer', 'width', 'feat'), may hold values from -0.125 to 0.125
- enc_bias: float32 [4, 8192], P('layer', 'feat'), may hold values from -3 to 3
- dec_weight: bfloat16 [4, 4, 8192, 2304], P('layer', None, 'feat', 'width'), may hold values from -0.0625 to 0.0625
- active: int32 [4, 1024, 8192], P('layer', None, 'feat'), may hold values 0 or 1
Outputs:
- dec_grad: bfloat16 [4, 4, 8192, 2304], P('layer', None, 'feat', 'width')
- enc_grad: bfloat16 [4, 2304, 8192], P('layer', 'width', 'feat')
- bias_grad: float32 [4, 8192], P('layer', 'feat')
- feat_grad: bfloat16 [4, 1024, 8192], P('layer', None, 'feat')
The draws below stay inside these ranges and needn't reach their ends.
All inputs are finite; a program needn't handle non-finite values. No bound on the sum of `active` on one device may be relied on, other than what follows from the above.
Results may differ from the reference program's by a relative error of at most 0.005.
Values may be sent and summed in bfloat16 or wider, within the bound.
A program may use at most 64 MiB of HBM per device.

```python
import jax
import jax.numpy as jnp
from jax import lax

D = 2304
FEAT = 8192
LAYERS = 4
TOKENS = 1024


def set_ends(drawn, rng, smallest, largest):
    longest = drawn.shape.index(max(drawn.shape))
    spots = []
    for shift in (0, 1):
        where = [jax.random.randint(jax.random.fold_in(rng, axis), (), 0, length) for axis, length in enumerate(drawn.shape)]
        where[longest] = (where[longest] + shift) % drawn.shape[longest]
        spots.append(tuple(where))
    return drawn.at[spots[0]].set(smallest).at[spots[1]].set(largest)


def steps_of(own_key, dims, cuts, smallest, top_value):
    def one(dim, parts):
        heights = jax.random.uniform(jax.random.fold_in(jax.random.fold_in(own_key, 6), dim), (parts,), jnp.float32, smallest / len(cuts), top_value / len(cuts))
        return jnp.repeat(jnp.exp(heights), dims[dim] // parts).reshape((-1,) + (1,) * (len(dims) - dim - 1))

    gain = one(*cuts[0])
    for cut in cuts[1:]:
        gain = gain * one(*cut)
    return gain


def gaussian(key, extent, scale, most, shards=(), dtype=jnp.bfloat16):
    entries = jax.random.normal(key, extent, jnp.float32) * scale
    if len(shards) > 0:
        entries = steps_of(key, extent, shards, -0.22, 0.18) * entries
    return jnp.clip(entries, min=-most, max=most).astype(dtype)


def setup_inputs(seed: int = 0) -> dict:
    key_list = jax.random.split(jax.random.key(seed), 7)
    residuals = gaussian(key_list[0], (LAYERS, TOKENS, D), 1.0, 6.0, ((0, 4), (1, 32), (2, 4)))
    cotangent = gaussian(key_list[1], (LAYERS, TOKENS, D), 1.0, 6.0, ((0, 4), (1, 32), (2, 4)))
    enc_weight = gaussian(key_list[2], (LAYERS, D, FEAT), D ** -0.5, 0.125, ((0, 4), (1, 4), (2, 32)))
    enc_bias = gaussian(key_list[3], (LAYERS, FEAT), 0.5, 3.0, ((0, 4), (1, 32)), jnp.float32)
    dec_weight = gaussian(key_list[4], (LAYERS, LAYERS, FEAT, D), FEAT ** -0.5, 0.0625, ((0, 4), (2, 32), (3, 4)))
    active = set_ends((jax.random.randint(key_list[5], (LAYERS, TOKENS, FEAT), 0, 2) < 1).astype(jnp.int32), jax.random.fold_in(key_list[5], 1), 0, 1)
    return {"residuals": residuals, "cotangent": cotangent, "enc_weight": enc_weight, "enc_bias": enc_bias, "dec_weight": dec_weight, "active": active}


def reference(residuals, cotangent, enc_weight, enc_bias, dec_weight, active):
    layers = residuals.shape[0]
    dec_rows = []
    enc_rows = []
    bias_rows = []
    feat_rows = []
    for source in range(layers):
        gate_all = active[source].astype(jnp.float32)
        pre_act = jnp.dot(residuals[source], enc_weight[source], preferred_element_type=jnp.float32) + enc_bias[source]
        activation = (pre_act * gate_all).astype(jnp.bfloat16)
        act_grad = jnp.zeros(gate_all.shape, jnp.float32)
        blocks = []
        for target in range(layers):
            if target < source:
                blocks.append(jnp.zeros(dec_weight.shape[2:], jnp.bfloat16))
            else:
                outer = lax.dot_general(activation, cotangent[target], (((0,), (0,)), ((), ())), preferred_element_type=jnp.float32)
                blocks.append(outer.astype(jnp.bfloat16))
                act_grad = act_grad + lax.dot_general(cotangent[target], dec_weight[source, target], (((1,), (1,)), ((), ())), preferred_element_type=jnp.float32)
        feat_grad = (act_grad * gate_all).astype(jnp.bfloat16)
        enc_grad = lax.dot_general(residuals[source], feat_grad, (((0,), (0,)), ((), ())), preferred_element_type=jnp.float32)
        dec_rows.append(jnp.stack(blocks))
        enc_rows.append(enc_grad.astype(jnp.bfloat16))
        bias_rows.append(jnp.sum(feat_grad.astype(jnp.float32), axis=0))
        feat_rows.append(feat_grad)
    return (jnp.stack(dec_rows), jnp.stack(enc_rows), jnp.stack(bias_rows), jnp.stack(feat_rows))
```

```python
import jax
import jax.numpy as jnp
from jax import lax
from jax.experimental import pallas as pl
from jax.experimental.pallas import tpu as pltpu
from jax.sharding import PartitionSpec as P

MESH = pl.DeviceIdType.MESH
BF16, F32 = jnp.bfloat16, jnp.float32

NX, NZ, NJ = 4, 8, 4
TOK = 32
ROWS = NJ * TOK
HALF = ROWS // 2
D = 576
PAD = 640
OFF = PAD - D
FEATS = 256
T_HOPS = 2


def nt(a, b):
    return lax.dot_general(a, b, (((1,), (1,)), ((), ())), preferred_element_type=F32)


def tn(a, b):
    return lax.dot_general(a, b, (((0,), (0,)), ((), ())), preferred_element_type=F32)


def kernel(
    resid, cot, bias, encw_hbm, decw_hbm, active_hbm,
    dec_out, enc_out, bias_out, fg_out,
    gp, cots, encw, ew, decw, dw, active,
    part, r1, s2, r2, af,
    loc_sem, p_recv, c_recv, zp_send, zt_send, yp_send, yt_send, xs_send, tx_send,
    r_recv, r_send,
):
    x = lax.axis_index("layer")
    f = lax.axis_index("feat")
    w = lax.axis_index("width")
    z, j = lax.div(f, NJ), lax.rem(f, NJ)
    c = lax.rem(w, 2)

    def at(dx=0, zz=None, jj=None, ww=None):
        zz = z if zz is None else zz
        jj = j if jj is None else jj
        return {"layer": lax.rem(x + dx, NX), "feat": zz * NJ + jj, "width": w if ww is None else ww}

    zi = lambda d: lax.rem(z + d + NZ, NZ)
    up, down = at(zz=zi(1)), at(zz=zi(-1))
    core_peer = at(ww=w + 1 - 2 * c)
    far_peer = at(ww=lax.rem(w + 2, 4))
    y_next, y_prev = at(jj=j + 1), at(jj=j - 1)
    o1 = jnp.where(j == 0, 1, j - 1)
    o2 = jnp.where(j == 0, 2, jnp.where(j == 3, 1, j + 1))
    o3 = jnp.where(j < 2, 3, 0)
    order = [j, o1, o2, o3]

    loads = [
        (pltpu.make_async_copy(encw_hbm.at[0], encw, loc_sem.at[4]), None),
        (pltpu.make_async_copy(active_hbm.at[0], active, loc_sem.at[5]), None),
    ]
    for k in range(NX):
        loads.append((pltpu.make_async_copy(decw_hbm.at[0, jnp.minimum(x + k, NX - 1)], decw.at[k], loc_sem.at[k]), x + k < NX))
    for cp, cond in loads:
        if cond is None:
            cp.start()
        else:
            pl.when(cond)(cp.start)

    barrier = pltpu.get_barrier_semaphore()

    def greet(dev):
        pl.semaphore_signal(barrier, inc=1, device_id=dev, device_id_type=MESH)

    for dev in (core_peer, far_peer, up, down, at(1), at(2), at(3)):
        greet(dev)
    pl.when(j < NJ - 1)(lambda: greet(y_next))
    pl.when(j > 0)(lambda: greet(y_prev))
    gp[f] = jnp.concatenate([resid[0], cot[0]], axis=1)
    pl.semaphore_wait(barrier, 7 + (j > 0).astype(jnp.int32) + (j < NJ - 1).astype(jnp.int32))

    def remote(src, dst, ss, rs, dev):
        return pltpu.make_async_remote_copy(src, dst, ss, rs, device_id=dev, device_id_type=MESH)

    sent = []

    def send(cp, cond=None):
        sent.append((cp, cond))
        if cond is None:
            cp.start()
        else:
            pl.when(cond)(cp.start)

    own_cot = lambda fi: gp.at[fi, :, pl.ds(2 * D - PAD, PAD)]

    def send_z(fi, d, cond=None):
        send(remote(gp.at[fi], gp.at[fi], zp_send.at[d, fi], p_recv.at[fi], (up, down)[d]), cond)

    def send_zt(fi, d, cond):
        send(remote(cots.at[1, fi], cots.at[1, fi], zt_send.at[d, fi], c_recv.at[1, fi], (up, down)[d]), cond)

    def send_x(fi):
        send(remote(own_cot(fi), cots.at[0, fi], xs_send.at[0, fi], c_recv.at[0, fi], at(3)), x >= 1)
        send(remote(own_cot(fi), cots.at[2, fi], xs_send.at[1, fi], c_recv.at[2, fi], at(1)), x == 3)

    def wait_p(fi):
        remote(gp.at[fi], gp.at[fi], zp_send.at[0, fi], p_recv.at[fi], up).wait_recv()

    def wait_c(k, fi):
        remote(cots.at[k, fi], cots.at[k, fi], zp_send.at[0, fi], c_recv.at[k, fi], up).wait_recv()

    for d in (0, 1):
        send_z(f, d)
    send(remote(gp.at[f], gp.at[f], yp_send.at[0, j], p_recv.at[f], y_next), j < NJ - 1)
    send(remote(gp.at[f], gp.at[f], yp_send.at[1, j], p_recv.at[f], y_prev), j > 0)
    send(remote(own_cot(f), cots.at[1, f], tx_send.at[f], c_recv.at[1, f], at(2)), x >= 2)
    send_x(f)

    third = x <= 1

    def ev_t_own():
        pl.when(third)(lambda: wait_c(1, f))
        for d in (0, 1):
            send_zt(f, d, third)
        send(remote(cots.at[1, f], cots.at[1, f], yt_send.at[0, j], c_recv.at[1, f], y_next), third & (j < NJ - 1))
        send(remote(cots.at[1, f], cots.at[1, f], yt_send.at[1, j], c_recv.at[1, f], y_prev), third & (j > 0))

    def ev_y(i):
        oi = order[i]
        fi = z * NJ + oi
        wait_p(fi)
        send(remote(gp.at[fi], gp.at[fi], yp_send.at[0, oi], p_recv.at[fi], y_next), (oi < j) & (j < NJ - 1))
        send(remote(gp.at[fi], gp.at[fi], yp_send.at[1, oi], p_recv.at[fi], y_prev), (oi > j) & (j > 0))
        for d in (0, 1):
            send_z(fi, d)
        send_x(fi)

    def ev_yt(i):
        oi = order[i]
        fi = z * NJ + oi
        pl.when(third)(lambda: wait_c(1, fi))
        send(remote(cots.at[1, fi], cots.at[1, fi], yt_send.at[0, oi], c_recv.at[1, fi], y_next), third & (oi < j) & (j < NJ - 1))
        send(remote(cots.at[1, fi], cots.at[1, fi], yt_send.at[1, oi], c_recv.at[1, fi], y_prev), third & (oi > j) & (j > 0))
        for d in (0, 1):
            send_zt(fi, d, third)

    def ev_z(r, i, d):
        fi = zi(-r if d == 0 else r) * NJ + order[i]
        wait_p(fi)
        if r < 3 or (r == 3 and (i < 2) == (d == 0)):
            send_z(fi, d)
        send_x(fi)

    def ev_zt(r, i, d):
        fi = zi(-r if d == 0 else r) * NJ + order[i]
        pl.when(third)(lambda: wait_c(1, fi))
        if r < T_HOPS:
            send_zt(fi, d, third)

    relay = (x == 1) | (x == 2)
    waited_a = set()

    def ev_relay(r, i, sgn):
        fi = zi(sgn * r) * NJ + order[i]
        pl.when(relay)(lambda: wait_c(0, fi))
        send(remote(cots.at[0, fi], cots.at[1, fi], tx_send.at[fi], c_recv.at[1, fi], at(3)), relay)

    def setup():
        for cp, cond in loads:
            if cond is None:
                cp.wait()
            else:
                pl.when(cond)(cp.wait)
        ew[0:D, :] = encw[...]
        ew[D:PAD, :] = jnp.zeros((OFF, FEATS), BF16)
        for k in range(NX):
            @pl.when(x + k < NX)
            def _():
                dw[k] = jnp.concatenate([jnp.zeros((FEATS, OFF), BF16), decw[k]], axis=1)

    def block(zz):
        rows = gp.at[pl.ds(zz * NJ, NJ)]
        part[zz, 0] = jnp.dot(rows[:, :, 0:PAD].reshape(ROWS, PAD), ew[...], preferred_element_type=F32)
        part[zz, 1] = nt(rows[:, :, 2 * D - PAD :].reshape(ROWS, PAD), dw[0])

    def block_c(zz, k, cond):
        @pl.when(cond)
        def _():
            part[zz, 1] += nt(cots[k, pl.ds(zz * NJ, NJ)].reshape(ROWS, PAD), dw[k + 1])

    def wait_block(zz, d):
        for i in range(NJ):
            fi = zz * NJ + order[i]
            if abs(d) > T_HOPS:
                pl.when(x == 0)(lambda: wait_c(0, fi))
                pl.when(third)(lambda: wait_c(1, fi))
            else:
                pl.when(x <= 2)(lambda: wait_c(0, fi))
            pl.when(x == 0)(lambda: wait_c(2, fi))

    mine = pl.ds(pl.multiple_of(c * HALF, HALF), HALF)
    other = pl.ds(pl.multiple_of((1 - c) * HALF, HALF), HALF)

    def red1(zz):
        send(remote(part.at[zz, :, other], r1.at[zz], r_send.at[0, zz], r_recv.at[0, zz], core_peer))

    def red2(zz):
        remote(part.at[zz, :, other], r1.at[zz], r_send.at[0, zz], r_recv.at[0, zz], core_peer).wait_recv()
        s2[zz] = (part[zz, :, mine, :] + r1[zz]).astype(BF16)
        send(remote(s2.at[zz], r2.at[zz], r_send.at[1, zz], r_recv.at[1, zz], far_peer))

    def red3(zz):
        remote(s2.at[zz], r2.at[zz], r_send.at[1, zz], r_recv.at[1, zz], far_peer).wait_recv()
        total = s2[zz].astype(F32) + r2[zz].astype(F32)
        rows = pl.ds(pl.multiple_of(zz * ROWS + c * HALF, HALF), HALF)
        gate = active[rows, :].astype(F32)
        af[0, rows, :] = ((total[0] + bias[...]) * gate).astype(BF16)
        af[1, rows, :] = (total[1] * gate).astype(BF16)
        send(remote(af.at[:, rows], af.at[:, rows], r_send.at[2, zz], r_recv.at[2, zz], core_peer))

    def red4(zz):
        rows = pl.ds(pl.multiple_of(zz * ROWS + (1 - c) * HALF, HALF), HALF)
        remote(af.at[:, rows], af.at[:, rows], r_send.at[2, zz], r_recv.at[2, zz], core_peer).wait_recv()

    def compute(d):
        zz = zi(d)
        wait_block(zz, d)
        block(zz)
        block_c(zz, 0, x <= 2)
        block_c(zz, 1, x <= 1)
        block_c(zz, 2, x == 0)
        red1(zz)

    setup()
    ev_t_own()
    for i in (1, 2, 3):
        ev_y(i)
        ev_yt(i)
    for i in range(NJ):
        for d in (0, 1):
            ev_z(1, i, d)
            ev_zt(1, i, d)
    compute(0)
    for i in range(NJ):
        for d in (0, 1):
            ev_z(2, i, d)
            ev_zt(2, i, d)
    compute(-1)
    compute(1)
    red2(zi(0))
    for i in range(NJ):
        for d in (0, 1):
            ev_z(3, i, d)
    red2(zi(-1))
    red2(zi(1))
    red3(zi(0))
    compute(-2)
    compute(2)
    for i in range(NJ):
        ev_relay(3, i, -1)
        ev_relay(3, i, 1)
    for i in range(NJ):
        ev_z(4, i, 0 if i < 2 else 1)
    for d in (-1, 1):
        red3(zi(d))
    for d in (-2, 2):
        red2(zi(d))
    compute(-3)
    compute(3)
    for d in (-2, 2):
        red3(zi(d))
    for i in range(NJ):
        ev_relay(4, i, 1)
    compute(4)
    for d in (-3, 3, 4):
        red2(zi(d))
    for d in (-3, 3, 4):
        red3(zi(d))
    for d in (0, -1, 1, -2, 2, -3, 3, 4):
        red4(zi(d))

    act = af[0]
    fg = af[1]
    for t in range(NX):
        @pl.when(t < x)
        def _():
            dec_out[0, t] = jnp.zeros((FEATS, D), BF16)

    tokens = NZ * ROWS
    dec_out[0, x] = tn(act, gp[:, :, 2 * D - PAD :].reshape(tokens, PAD))[:, OFF:].astype(BF16)
    for k in range(NX - 1):
        @pl.when(x + k + 1 < NX)
        def _():
            dec_out[0, x + k + 1] = tn(act, cots[k].reshape(tokens, PAD))[:, OFF:].astype(BF16)
    enc_out[0] = tn(gp[:, :, 0:PAD].reshape(tokens, PAD), fg)[0:D, :].astype(BF16)
    bias_out[...] = jnp.sum(fg.astype(F32), axis=0, keepdims=True)
    fg_out[0] = fg

    for cp, cond in sent:
        if cond is None:
            cp.wait_send()
        else:
            pl.when(cond)(cp.wait_send)


def local(residuals, cotangent, enc_weight, enc_bias, dec_weight, active):
    vmem, hbm = pl.BlockSpec(memory_space=pltpu.VMEM), pl.BlockSpec(memory_space=pl.ANY)
    chunks, dma = NZ * NJ, pltpu.SemaphoreType.DMA
    return pl.pallas_call(
        kernel,
        out_shape=(
            jax.ShapeDtypeStruct((1, NX, FEATS, D), BF16),
            jax.ShapeDtypeStruct((1, D, FEATS), BF16),
            jax.ShapeDtypeStruct((1, FEATS), F32),
            jax.ShapeDtypeStruct((1, NZ * ROWS, FEATS), BF16),
        ),
        in_specs=[vmem, vmem, vmem, hbm, hbm, hbm],
        out_specs=(vmem, vmem, vmem, vmem),
        scratch_shapes=[
            pltpu.VMEM((chunks, TOK, 2 * D), BF16),
            pltpu.VMEM((3, chunks, TOK, PAD), BF16),
            pltpu.VMEM((D, FEATS), BF16),
            pltpu.VMEM((PAD, FEATS), BF16),
            pltpu.VMEM((NX, FEATS, D), BF16),
            pltpu.VMEM((NX, FEATS, PAD), BF16),
            pltpu.VMEM((NZ * ROWS, FEATS), jnp.int32),
            pltpu.VMEM((NZ, 2, ROWS, FEATS), F32),
            pltpu.VMEM((NZ, 2, HALF, FEATS), F32),
            pltpu.VMEM((NZ, 2, HALF, FEATS), BF16),
            pltpu.VMEM((NZ, 2, HALF, FEATS), BF16),
            pltpu.VMEM((2, NZ * ROWS, FEATS), BF16),
            dma((6,)),
            dma((chunks,)),
            dma((3, chunks)),
            dma((2, chunks)),
            dma((2, chunks)),
            dma((2, NJ)),
            dma((2, NJ)),
            dma((2, chunks)),
            dma((chunks,)),
            dma((3, NZ)),
            dma((3, NZ)),
        ],
        compiler_params=pltpu.CompilerParams(collective_id=0, has_side_effects=True, vmem_limit_bytes=60 * 2**20),
    )(residuals, cotangent, enc_bias, enc_weight, dec_weight, active)


def solution(mesh):
    in_specs = (
        P("layer", "feat", "width"),
        P("layer", "feat", "width"),
        P("layer", "width", "feat"),
        P("layer", "feat"),
        P("layer", None, "feat", "width"),
        P("layer", None, "feat"),
    )
    out_specs = (
        P("layer", None, "feat", "width"),
        P("layer", "width", "feat"),
        P("layer", "feat"),
        P("layer", None, "feat"),
    )
    return jax.shard_map(local, mesh=mesh, in_specs=in_specs, out_specs=out_specs, check_vma=False)
```

```python
import jax
import jax.numpy as jnp
from jax import lax
from jax.experimental import pallas as pl
from jax.experimental.pallas import tpu as pltpu
from jax.sharding import PartitionSpec as P

MESH = pl.DeviceIdType.MESH
BF16, F32 = jnp.bfloat16, jnp.float32

NX, NZ, NJ = 4, 8, 4
TOK = 32
ROWS = NJ * TOK
HALF = ROWS // 2
D = 576
PAD = 640
OFF = PAD - D
FEATS = 256
LAST = NZ - 1


def nn(a, b):
    return jnp.dot(a, b, preferred_element_type=F32)


def tn(a, b):
    return lax.dot_general(a, b, (((0,), (0,)), ((), ())), preferred_element_type=F32)


def kernel(
    resid, cot, bias, encw_hbm, decw_hbm, active_hbm,
    dec_out, enc_out, bias_out, fg_out,
    gp, cots, encw, ew, decw, dw, active,
    part, r1, s2, r2, af, acc, dec_st, enc_st,
    loc_sem, out_sem, p_recv, c_recv, zp_send, zt_send, yp_send, yt_send, xs_send, tx_send,
    r_recv, r_send,
):
    x = lax.axis_index("layer")
    f = lax.axis_index("feat")
    w = lax.axis_index("width")
    z, j = lax.div(f, NJ), lax.rem(f, NJ)
    c = lax.rem(w, 2)

    def at(dx=0, zz=None, jj=None, ww=None):
        zz = z if zz is None else zz
        jj = j if jj is None else jj
        return {"layer": lax.rem(x + dx, NX), "feat": zz * NJ + jj, "width": w if ww is None else ww}

    zi = lambda d: lax.rem(z + d + NZ, NZ)
    hop = (at(zz=zi(1)), at(zz=zi(-1)))
    core_peer = at(ww=w + 1 - 2 * c)
    far_peer = at(ww=lax.rem(w + 2, 4))
    order = [
        j,
        jnp.where(j == 0, 1, j - 1),
        jnp.where(j == 0, 2, jnp.where(j == 3, 1, j + 1)),
        jnp.where(j < 2, 3, 0),
    ]

    slot = lambda d: d + 3
    chunk = lambda d, i: slot(d) * NJ + order[i]

    def when(cond, fn):
        if cond is None:
            fn()
        else:
            pl.when(cond)(fn)

    loads = [
        (pltpu.make_async_copy(encw_hbm.at[0], encw, loc_sem.at[4]), None),
        (pltpu.make_async_copy(active_hbm.at[0], active, loc_sem.at[5]), None),
    ]
    for k in range(NX):
        loads.append((pltpu.make_async_copy(decw_hbm.at[0, jnp.minimum(x + k, NX - 1)], decw.at[k], loc_sem.at[k]), x + k < NX))

    barrier = pltpu.get_barrier_semaphore()
    peers = [core_peer, far_peer, hop[0], hop[1], at(1), at(2), at(3)] + [at(jj=order[i]) for i in (1, 2, 3)]
    for dev in peers:
        pl.semaphore_signal(barrier, inc=1, device_id=dev, device_id_type=MESH)
    gp[chunk(0, 0)] = jnp.concatenate([resid[0], cot[0]], axis=1)
    for cp, cond in loads:
        when(cond, cp.start)
    pl.semaphore_wait(barrier, len(peers))

    def remote(src, dst, ss, rs, dev):
        return pltpu.make_async_remote_copy(src, dst, ss, rs, device_id=dev, device_id_type=MESH)

    sent = []

    def send(cp, cond=None):
        sent.append((cp, cond))
        when(cond, cp.start)

    third = x <= 1
    relay = (x == 1) | (x == 2)

    def next_d(r, d):
        return 4 if r == 3 else (r + 1 if d else -r - 1)

    def here(r, d):
        return 4 if r == 4 else (r if d else -r)

    def send_z(r, i, d):
        a, b = chunk(here(r, d), i), chunk(next_d(r, d), i)
        send(remote(gp.at[a], gp.at[b], zp_send.at[d, a], p_recv.at[b], hop[d]))

    def send_zt(r, i, d):
        a, b = chunk(here(r, d), i), chunk(next_d(r, d), i)
        send(remote(cots.at[1, a], cots.at[1, b], zt_send.at[d, a], c_recv.at[1, b], hop[d]), third)

    def send_x(a):
        own = gp.at[a, :, pl.ds(2 * D - PAD, PAD)]
        send(remote(own, cots.at[0, a], xs_send.at[0, a], c_recv.at[0, a], at(3)), x >= 1)
        send(remote(own, cots.at[2, a], xs_send.at[1, a], c_recv.at[2, a], at(1)), x == 3)

    def wait_p(a):
        remote(gp.at[a], gp.at[a], zp_send.at[0, a], p_recv.at[a], hop[0]).wait_recv()

    def wait_c(k, a, cond):
        cp = remote(cots.at[k, a], cots.at[k, a], zp_send.at[0, a], c_recv.at[k, a], hop[0])
        when(cond, cp.wait_recv)

    def own():
        a = chunk(0, 0)
        for d in (0, 1):
            send_z(0, 0, d)
        for i in (1, 2, 3):
            send(remote(gp.at[a], gp.at[a], yp_send.at[i], p_recv.at[a], at(jj=order[i])))
        send(remote(gp.at[a, :, pl.ds(2 * D - PAD, PAD)], cots.at[1, a], tx_send.at[a], c_recv.at[1, a], at(2)), x >= 2)
        send_x(a)

    def t0():
        a = chunk(0, 0)
        wait_c(1, a, third)
        for i in (1, 2, 3):
            send(remote(cots.at[1, a], cots.at[1, a], yt_send.at[i], c_recv.at[1, a], at(jj=order[i])), third)

    def y(i):
        a = chunk(0, i)
        wait_p(a)
        for d in (0, 1):
            send_z(0, i, d)
        send_x(a)

    def ty(i):
        wait_c(1, chunk(0, i), third)
        for d in (0, 1):
            send_zt(0, i, d)

    def zp(r, i):
        for d in (0, 1):
            if r == 4 and (i < 2) != (d == 0):
                continue
            a = chunk(here(r, d), i)
            wait_p(a)
            if r < 3 or (r == 3 and (i < 2) == (d == 0)):
                send_z(r, i, d)
            send_x(a)

    def zt(r, i):
        for d in (0, 1):
            if r == 4 and (i == 1) != (d == 0):
                continue
            wait_c(1, chunk(here(r, d), i), third)
            if r < 3 or (r == 3 and (i == 1) == (d == 0)):
                send_zt(r, i, d)

    def rl(r):
        for d in (-r, r) if r < 4 else (4,):
            a = chunk(d, 0)
            wait_c(0, a, relay)
            send(remote(cots.at[0, a], cots.at[1, a], tx_send.at[a], c_recv.at[1, a], at(3)), relay)

    def setup():
        for cp, cond in loads:
            when(cond, cp.wait)
        ew[0:D, :] = encw[...]
        ew[D:PAD, :] = jnp.zeros((OFF, FEATS), BF16)
        for k in range(NX):
            @pl.when(x + k < NX)
            def _():
                dw[k, 0:OFF, :] = jnp.zeros((OFF, FEATS), BF16)
                dw[k, OFF:PAD, :] = decw[k]
        for t in range(NX):
            @pl.when(t < x)
            def _():
                dec_st[t] = jnp.zeros((D, FEATS), BF16)

    def compute(d):
        for i in range(NJ):
            a = chunk(d, i)
            wait_c(0, a, x == 0 if i == 0 and d != 0 else x <= 2)
            if i == 0 and d != 0:
                wait_c(1, a, third)
            wait_c(2, a, x == 0)
        s = slot(d)
        at_s = slice(s * NJ, (s + 1) * NJ)
        rows = gp[at_s]
        part[s, 0] = nn(rows[:, :, 0:PAD].reshape(ROWS, PAD), ew[...])
        part[s, 1] = nn(rows[:, :, 2 * D - PAD :].reshape(ROWS, PAD), dw[0])
        for k, cond in enumerate((x <= 2, x <= 1, x == 0)):
            @pl.when(cond)
            def _():
                part[s, 1] += nn(cots[k, at_s].reshape(ROWS, PAD), dw[k + 1])
        send(sum1(s))

    mine = pl.ds(pl.multiple_of(c * HALF, HALF), HALF)
    other = pl.ds(pl.multiple_of((1 - c) * HALF, HALF), HALF)
    sum1 = lambda s: remote(part.at[s, :, other], r1.at[s], r_send.at[0, s], r_recv.at[0, s], core_peer)
    sum2 = lambda s: remote(s2.at[s], r2.at[s], r_send.at[1, s], r_recv.at[1, s], far_peer)

    def sum3(s, half):
        rows = pl.ds(pl.multiple_of(s * ROWS + half * HALF, HALF), HALF)
        return remote(af.at[:, rows], af.at[:, rows], r_send.at[2, s], r_recv.at[2, s], core_peer)

    def red2(d):
        s = slot(d)
        sum1(s).wait_recv()
        s2[s] = (part[s, :, mine, :] + r1[s]).astype(BF16)
        send(sum2(s))

    def red3(d):
        s = slot(d)
        sum2(s).wait_recv()
        total = s2[s].astype(F32) + r2[s].astype(F32)
        gate = active[pl.ds(pl.multiple_of(zi(d) * ROWS + c * HALF, HALF), HALF), :].astype(F32)
        rows = pl.ds(pl.multiple_of(s * ROWS + c * HALF, HALF), HALF)
        af[0, rows, :] = ((total[0] + bias[...]) * gate).astype(BF16)
        af[1, rows, :] = (total[1] * gate).astype(BF16)
        send(sum3(s, c))

    def fg_copy(d):
        s = slot(d)
        return pltpu.make_async_copy(
            af.at[1, s * ROWS : (s + 1) * ROWS],
            fg_out.at[0, pl.ds(pl.multiple_of(zi(d) * ROWS, ROWS), ROWS)],
            out_sem.at[s],
        )

    def red4(d):
        sum3(slot(d), 1 - c).wait_recv()
        fg_copy(d).start()

    def dec_copy(t):
        return pltpu.make_async_copy(dec_st.at[t], dec_out.at[0, t], out_sem.at[NZ + t])

    enc_copy = pltpu.make_async_copy(enc_st, enc_out.at[0], out_sem.at[NZ + NX])

    def final(last):
        s = slice(LAST if last else 0, NZ if last else LAST)
        ch, rows = slice(s.start * NJ, s.stop * NJ), slice(s.start * ROWS, s.stop * ROWS)
        n = rows.stop - rows.start
        act, fg = af[0, rows], af[1, rows]

        def dec(k, data):
            g = tn(data.reshape(n, PAD), act)[OFF:]
            if last:
                t = x + k
                dec_st[t] = (acc[k] + g).astype(BF16)
                dec_copy(t).start()
            else:
                acc[k] = g

        g = tn(gp[ch, :, 0:PAD].reshape(n, PAD), fg)[0:D]
        b = jnp.sum(fg.astype(F32), axis=0, keepdims=True)
        if last:
            enc_st[...] = (acc[NX] + g).astype(BF16)
            enc_copy.start()
            bias_out[...] += b
        else:
            acc[NX] = g
            bias_out[...] = b
        dec(0, gp[ch, :, 2 * D - PAD :])
        for k in range(1, NX):
            pl.when(x + k < NX)(lambda: dec(k, cots[k - 1, ch]))


    own()
    y(1), zp(1, 0), t0(), y(2), zp(1, 1), y(3)
    setup()
    for t in range(NX):
        pl.when(t < x)(lambda: dec_copy(t).start())
    ty(1), zp(1, 2), ty(2), zp(1, 3), ty(3), rl(1)
    zt(1, 1), zp(2, 0), compute(0), zt(1, 2), zp(2, 1), zt(1, 3), zp(2, 2), rl(2)
    red2(0), compute(-1), zt(2, 1), zp(2, 3), compute(1), zt(2, 2), zp(3, 0)
    red2(-1), red3(0), zt(2, 3), zp(3, 1), red2(1), compute(-2), rl(3), zt(3, 1), zp(3, 2)
    compute(2), red3(-1), zt(3, 2), zp(3, 3), red2(-2), red3(1), zp(4, 0), zp(4, 2), zt(3, 3)
    red2(2), compute(-3), rl(4), zp(4, 1), zp(4, 3), red3(-2), compute(3), red3(2)
    zt(4, 1), zt(4, 2), zt(4, 3)
    red2(-3), red2(3), compute(4), red3(-3), red3(3), red2(4)
    for d in range(-3, 4):
        red4(d)
    final(False)
    red3(4), red4(4)
    final(True)
    for cp, cond in sent:
        when(cond, cp.wait_send)
    for d in range(-3, 5):
        fg_copy(d).wait()
    for t in range(NX):
        dec_copy(t).wait()
    enc_copy.wait()


def local(residuals, cotangent, enc_weight, enc_bias, dec_weight, active):
    vmem, hbm = pl.BlockSpec(memory_space=pltpu.VMEM), pl.BlockSpec(memory_space=pl.ANY)
    chunks, dma = NZ * NJ, pltpu.SemaphoreType.DMA
    dec_grad, enc_grad, bias_grad, feat_grad = pl.pallas_call(
        kernel,
        out_shape=(
            jax.ShapeDtypeStruct((1, NX, D, FEATS), BF16),
            jax.ShapeDtypeStruct((1, D, FEATS), BF16),
            jax.ShapeDtypeStruct((1, FEATS), F32),
            jax.ShapeDtypeStruct((1, NZ * ROWS, FEATS), BF16),
        ),
        in_specs=[vmem, vmem, vmem, hbm, hbm, hbm],
        out_specs=(hbm, hbm, vmem, hbm),
        scratch_shapes=[
            pltpu.VMEM((chunks, TOK, 2 * D), BF16),
            pltpu.VMEM((3, chunks, TOK, PAD), BF16),
            pltpu.VMEM((D, FEATS), BF16),
            pltpu.VMEM((PAD, FEATS), BF16),
            pltpu.VMEM((NX, D, FEATS), BF16),
            pltpu.VMEM((NX, PAD, FEATS), BF16),
            pltpu.VMEM((NZ * ROWS, FEATS), jnp.int32),
            pltpu.VMEM((NZ, 2, ROWS, FEATS), F32),
            pltpu.VMEM((NZ, 2, HALF, FEATS), F32),
            pltpu.VMEM((NZ, 2, HALF, FEATS), BF16),
            pltpu.VMEM((NZ, 2, HALF, FEATS), BF16),
            pltpu.VMEM((2, NZ * ROWS, FEATS), BF16),
            pltpu.VMEM((NX + 1, D, FEATS), F32),
            pltpu.VMEM((NX, D, FEATS), BF16),
            pltpu.VMEM((D, FEATS), BF16),
            dma((6,)),
            dma((NZ + NX + 1,)),
            dma((chunks,)),
            dma((3, chunks)),
            dma((2, chunks)),
            dma((2, chunks)),
            dma((NJ,)),
            dma((NJ,)),
            dma((2, chunks)),
            dma((chunks,)),
            dma((3, NZ)),
            dma((3, NZ)),
        ],
        compiler_params=pltpu.CompilerParams(collective_id=0, has_side_effects=True, vmem_limit_bytes=60 * 2**20),
    )(residuals, cotangent, enc_bias, enc_weight, jnp.swapaxes(dec_weight, 2, 3), active)
    return jnp.swapaxes(dec_grad, 2, 3), enc_grad, bias_grad, feat_grad


def solution(mesh):
    in_specs = (
        P("layer", "feat", "width"),
        P("layer", "feat", "width"),
        P("layer", "width", "feat"),
        P("layer", "feat"),
        P("layer", None, "feat", "width"),
        P("layer", None, "feat"),
    )
    out_specs = (
        P("layer", None, "feat", "width"),
        P("layer", "width", "feat"),
        P("layer", "feat"),
        P("layer", None, "feat"),
    )
    return jax.shard_map(local, mesh=mesh, in_specs=in_specs, out_specs=out_specs, check_vma=False)
```

```python
import jax
import jax.numpy as jnp
from jax import lax
from jax.experimental import pallas as pl
from jax.experimental.pallas import tpu as pltpu
from jax.sharding import PartitionSpec as P

MESH = pl.DeviceIdType.MESH
BF16, F32 = jnp.bfloat16, jnp.float32

NX, NZ, NJ = 4, 8, 4
TOK = 32
SUB = TOK // 2
HALF = NJ * SUB
D = 576
MAIN = 512
TAIL = D - MAIN
WIDE = 2 * D
FEATS = 256
CHUNKS = NZ * NJ
LAST = NZ - 1


def nn(a, b):
    return jnp.dot(a, b, preferred_element_type=F32)


def tn(a, b):
    return lax.dot_general(a, b, (((0,), (0,)), ((), ())), preferred_element_type=F32)


def gather_kernel(
    resid_hbm, cot_hbm, bias_hbm, encw_hbm, decw_hbm, active_hbm,
    dec_out, enc_out, bias_out, fg_out,
    raw, gp, cots, weight, wtail, bias, active,
    part, r1, s2, r2, af, acc, bias_acc,
    loc_sem, p_recv, c_recv, zp_send, zt_send, yp_send, yt_send, xs_send, tx_send,
    r_recv, r_send,
):
    x = lax.axis_index("layer")
    f = lax.axis_index("feat")
    w = lax.axis_index("width")
    z, j = lax.div(f, NJ), lax.rem(f, NJ)
    c = lax.rem(w, 2)

    def at(dx=0, zz=None, jj=None, ww=None):
        zz = z if zz is None else zz
        jj = j if jj is None else jj
        return {"layer": lax.rem(x + dx, NX), "feat": zz * NJ + jj, "width": w if ww is None else ww}

    zi = lambda d: lax.rem(z + d + NZ, NZ)
    hop = (at(zz=zi(1)), at(zz=zi(-1)))
    core_peer = at(ww=w + 1 - 2 * c)
    far_peer = at(ww=lax.rem(w + 2, 4))
    order = [
        j,
        jnp.where(j == 0, 1, j - 1),
        jnp.where(j == 0, 2, jnp.where(j == 3, 1, j + 1)),
        jnp.where(j < 2, 3, 0),
    ]

    slot = lambda d: d + 3
    chunk = lambda d, i: slot(d) * NJ + order[i]

    def when(cond, fn):
        if cond is None:
            fn()
        else:
            pl.when(cond)(fn)

    barrier = pltpu.get_barrier_semaphore()
    peers = [core_peer, far_peer, hop[0], hop[1], at(1), at(2), at(3)] + [at(jj=order[i]) for i in (1, 2, 3)]
    for dev in peers:
        pl.semaphore_signal(barrier, inc=1, device_id=dev, device_id_type=MESH)

    first = [
        pltpu.make_async_copy(resid_hbm.at[0], raw.at[0], loc_sem.at[0]),
        pltpu.make_async_copy(cot_hbm.at[0], raw.at[1], loc_sem.at[1]),
    ]
    for cp in first:
        cp.start()
    loads = [
        (pltpu.make_async_copy(encw_hbm.at[0], weight.at[0], loc_sem.at[2]), None),
        (pltpu.make_async_copy(active_hbm.at[:, c], active, loc_sem.at[3]), None),
        (pltpu.make_async_copy(bias_hbm, bias, loc_sem.at[4]), None),
    ]
    for k in range(NX):
        cp = pltpu.make_async_copy(decw_hbm.at[0, jnp.minimum(x + k, NX - 1)], weight.at[k + 1], loc_sem.at[5 + k])
        loads.append((cp, x + k < NX))
    for cp, cond in loads:
        when(cond, cp.start)

    mine = chunk(0, 0)
    for u in (0, 1):
        first[u].wait()
        rows = raw[u]
        gp[mine, u, :, 0:MAIN] = rows[0:SUB, 0:MAIN]
        gp[mine, u, :, MAIN : 2 * MAIN] = rows[SUB:TOK, 0:MAIN]
        gp[mine, u, :, 2 * MAIN : WIDE] = jnp.concatenate([rows[0:SUB, MAIN:D], rows[SUB:TOK, MAIN:D]], axis=1)
    pl.semaphore_wait(barrier, len(peers))

    def remote(src, dst, ss, rs, dev):
        return pltpu.make_async_remote_copy(src, dst, ss, rs, device_id=dev, device_id_type=MESH)

    sent = []

    def send(cp, cond=None):
        sent.append((cp, cond))
        when(cond, cp.start)

    third = x <= 1

    def next_d(r, d):
        return 4 if r == 3 else (r + 1 if d else -r - 1)

    def here(r, d):
        return 4 if r == 4 else (r if d else -r)

    def send_z(r, i, d):
        a, b = chunk(here(r, d), i), chunk(next_d(r, d), i)
        send(remote(gp.at[a], gp.at[b], zp_send.at[d, a], p_recv.at[b], hop[d]))

    def send_zt(r, i, d):
        a, b = chunk(here(r, d), i), chunk(next_d(r, d), i)
        send(remote(cots.at[1, a], cots.at[1, b], zt_send.at[d, a], c_recv.at[1, b], hop[d]), third)

    def send_x(a, i):
        own = gp.at[a, 1]
        send(remote(own, cots.at[0, a], xs_send.at[0, a], c_recv.at[0, a], at(3)), x >= 1)
        send(remote(own, cots.at[2, a], xs_send.at[1, a], c_recv.at[2, a], at(1)), x == 3)
        if i == 1:
            send(remote(own, cots.at[1, a], xs_send.at[1, a], c_recv.at[1, a], at(1)), x == 2)

    def wait_p(a):
        remote(gp.at[a], gp.at[a], zp_send.at[0, a], p_recv.at[a], hop[0]).wait_recv()

    def wait_c(k, a, cond):
        cp = remote(cots.at[k, a], cots.at[k, a], zp_send.at[0, a], c_recv.at[k, a], hop[0])
        when(cond, cp.wait_recv)

    def own():
        for d in (0, 1):
            send_z(0, 0, d)
        send(remote(gp.at[mine, 1], cots.at[1, mine], tx_send.at[mine], c_recv.at[1, mine], at(2)), x >= 2)
        for i in (1, 2, 3):
            send(remote(gp.at[mine], gp.at[mine], yp_send.at[i], p_recv.at[mine], at(jj=order[i])))
        send_x(mine, 0)

    def t0():
        wait_c(1, mine, third)
        for i, cond in ((1, j >= 2), (2, (j == 0) | (j == 3)), (3, None)):
            cp = remote(cots.at[1, mine], cots.at[1, mine], yt_send.at[i], c_recv.at[1, mine], at(jj=order[i]))
            send(cp, third if cond is None else third & cond)

    def y(i):
        a = chunk(0, i)
        wait_p(a)
        for d in (0, 1):
            send_z(0, i, d)
        send_x(a, i)

    def ty(i):
        wait_c(1, chunk(0, i), third)
        for d in (0, 1):
            send_zt(0, i, d)

    def zp(r, i):
        for d in (0, 1):
            if r == 4 and (i < 2) != (d == 0):
                continue
            a = chunk(here(r, d), i)
            wait_p(a)
            if r < 3 or (r == 3 and (i < 2) == (d == 0)):
                send_z(r, i, d)
            send_x(a, i)

    def zt(r, i):
        for d in (0, 1):
            if r == 4 and (i == 2) != (d == 0):
                continue
            wait_c(1, chunk(here(r, d), i), third)
            if r < 3 or (r == 3 and (i == 2) == (d == 0)):
                send_zt(r, i, d)

    def rl(r):
        def hand(k, a, cond, dx):
            wait_c(k, a, cond)
            send(remote(cots.at[k, a], cots.at[1, a], tx_send.at[a], c_recv.at[1, a], at(dx)), cond)

        for d in (0,) if r == 0 else (4,) if r == 4 else (-r, r):
            if d:
                hand(0, chunk(d, 0), x == 1, 3)
                hand(2, chunk(d, 0), x == 0, 1)
            hand(1, chunk(d, 1), x == 3, 1)
            hand(2, chunk(d, 1), x == 0, 1)

    def setup():
        for cp, cond in loads:
            when(cond, cp.wait)
        wtail[...] = jnp.zeros_like(wtail)
        for k in range(NX + 1):
            wtail[k, 0:TAIL, 0:FEATS] = weight[k, MAIN:D, :]
            wtail[k, TAIL : 2 * TAIL, FEATS : 2 * FEATS] = weight[k, MAIN:D, :]
        for t in range(NX):
            @pl.when(t < x)
            def _():
                dec_out[t] = jnp.zeros((D, FEATS), BF16)

    def compute(d):
        for i in range(NJ):
            a = chunk(d, i)
            wait_c(0, a, (x == 0) | (x == 2) if i == 0 and d else x <= 2)
            if i == 1 or (i == 0 and d):
                wait_c(1, a, third)
            if i > 1 or (i == 0 and d == 0):
                wait_c(2, a, x == 0)
        s = slot(d)
        ch = slice(s * NJ, (s + 1) * NJ)

        def times(data, k):
            both = jnp.concatenate(
                [data[:, :, 0:MAIN].reshape(HALF, MAIN), data[:, :, MAIN : 2 * MAIN].reshape(HALF, MAIN)], axis=0
            )
            main = nn(both, weight[k, 0:MAIN, :])
            tails = nn(data[:, :, 2 * MAIN :].reshape(HALF, 2 * TAIL), wtail[k])
            return main[0:HALF] + tails[:, 0:FEATS], main[HALF:] + tails[:, FEATS:]

        for k in (0, 1):
            part[s, 0, k], part[s, 1, k] = times(gp[ch, k], k)
        for k, cond in enumerate((x <= 2, x <= 1, x == 0)):
            @pl.when(cond)
            def _():
                a, b = times(cots[k, ch], k + 2)
                part[s, 0, 1] += a
                part[s, 1, 1] += b
        send(sum1(s))

    sum1 = lambda s: remote(part.at[s, 1 - c], r1.at[s], r_send.at[0, s], r_recv.at[0, s], core_peer)
    sum2 = lambda s: remote(s2.at[s], r2.at[s], r_send.at[1, s], r_recv.at[1, s], far_peer)

    def sum3(s, half):
        block = af.at[half, :, s * HALF : (s + 1) * HALF]
        return remote(block, block, r_send.at[2, s], r_recv.at[2, s], core_peer)

    def red2(d):
        s = slot(d)
        sum1(s).wait_recv()
        s2[s] = (part[s, c] + r1[s]).astype(BF16)
        send(sum2(s))

    def red3(d):
        s = slot(d)
        sum2(s).wait_recv()
        total = s2[s].astype(F32) + r2[s].astype(F32)
        gate = active[pl.ds(zi(d) * NJ, NJ)].reshape(HALF, FEATS).astype(F32)
        rows = slice(s * HALF, (s + 1) * HALF)
        af[c, 0, rows, :] = ((total[0] + bias[...]) * gate).astype(BF16)
        af[c, 1, rows, :] = (total[1] * gate).astype(BF16)
        send(sum3(s, c))

    def red4(d):
        s = slot(d)
        sum3(s, 1 - c).wait_recv()
        for h in (0, 1):
            fg_out[pl.ds(zi(d) * NJ, NJ), h] = af[h, 1, s * HALF : (s + 1) * HALF].reshape(NJ, SUB, FEATS)

    def final(last):
        lo, hi = (LAST, NZ) if last else (0, LAST)
        ch, rows = slice(lo * NJ, hi * NJ), slice(lo * HALF, hi * HALF)
        n = (hi - lo) * HALF

        def grads(data, k):
            a, b = af[0, k, rows], af[1, k, rows]
            main = tn(data[:, :, 0:MAIN].reshape(n, MAIN), a) + tn(data[:, :, MAIN : 2 * MAIN].reshape(n, MAIN), b)
            tails = data[:, :, 2 * MAIN :].reshape(n, 2 * TAIL)
            return main, tn(tails, a)[0:TAIL] + tn(tails, b)[TAIL:]

        def put(k, g, write):
            for piece, at_rows in zip(g, (slice(0, MAIN), slice(MAIN, D))):
                if last:
                    write(at_rows, (acc[k, at_rows] + piece).astype(BF16))
                else:
                    acc[k, at_rows] = piece

        def dec(k, data):
            def write(at_rows, v):
                dec_out[x + k, at_rows] = v

            put(k, grads(data, 0), write)

        def write_enc(at_rows, v):
            enc_out[at_rows] = v

        put(NX, grads(gp[ch, 0], 1), write_enc)
        sums = sum(jnp.sum(af[h, 1, rows].astype(F32), axis=0, keepdims=True) for h in (0, 1))
        if last:
            bias_out[...] = bias_acc[...] + sums
        else:
            bias_acc[...] = sums
        dec(0, gp[ch, 1])
        for k in range(1, NX):
            pl.when(x + k < NX)(lambda: dec(k, cots[k - 1, ch]))

    own()
    y(1), zp(1, 0), y(2), zp(1, 1), y(3), t0()
    setup()
    zp(1, 2), ty(2), rl(0), zp(1, 3), ty(3), zp(2, 0), rl(1), zp(2, 1), compute(0)
    zt(1, 2), zp(2, 2), zt(1, 3), compute(-1), zp(2, 3), red2(0), compute(1), rl(2)
    zp(3, 0), zt(2, 2), zp(3, 1), red2(-1), zt(2, 3), red2(1), compute(-2), zp(3, 2), compute(2)
    zp(3, 3), rl(3), zt(3, 2), red2(-2), zt(3, 3), zp(4, 0), zp(4, 2), red2(2), compute(-3)
    zp(4, 1), zp(4, 3), compute(3), rl(4), red2(-3), zt(4, 2), zt(4, 3), red2(3)
    compute(4), red3(0), red3(-1), red2(4)
    for d in (1, -2, 2, -3, 3):
        red3(d)
    for d in range(-3, 4):
        red4(d)
    final(False)
    red3(4), red4(4)
    final(True)
    for cp, cond in sent:
        when(cond, cp.wait_send)


def write_kernel(dec, enc, bias, fg, dec_out, enc_out, bias_out, fg_out, sem):
    copies = [
        pltpu.make_async_copy(dec, dec_out, sem.at[0]),
        pltpu.make_async_copy(enc, enc_out, sem.at[1]),
        pltpu.make_async_copy(bias, bias_out, sem.at[2]),
        pltpu.make_async_copy(fg, fg_out, sem.at[3]),
    ]
    for cp in copies:
        cp.start()
    for cp in copies:
        cp.wait()


def local(residuals, cotangent, enc_weight, enc_bias, dec_weight, active):
    vmem, hbm = pl.BlockSpec(memory_space=pltpu.VMEM), pl.BlockSpec(memory_space=pltpu.HBM)
    dma = pltpu.SemaphoreType.DMA
    outs = [((NX, D, FEATS), BF16), ((D, FEATS), BF16), ((1, FEATS), F32), ((CHUNKS, 2, SUB, FEATS), BF16)]
    held = pl.pallas_call(
        gather_kernel,
        out_shape=tuple(pltpu.VMEM(shape, dtype) for shape, dtype in outs),
        in_specs=[hbm] * 6,
        out_specs=(vmem,) * 4,
        scratch_shapes=[
            pltpu.VMEM((2, TOK, D), BF16),
            pltpu.VMEM((CHUNKS, 2, SUB, WIDE), BF16),
            pltpu.VMEM((3, CHUNKS, SUB, WIDE), BF16),
            pltpu.VMEM((NX + 1, D, FEATS), BF16),
            pltpu.VMEM((NX + 1, 2 * TAIL, 2 * FEATS), BF16),
            pltpu.VMEM((1, FEATS), F32),
            pltpu.VMEM((CHUNKS, SUB, FEATS), jnp.int32),
            pltpu.VMEM((NZ, 2, 2, HALF, FEATS), F32),
            pltpu.VMEM((NZ, 2, HALF, FEATS), F32),
            pltpu.VMEM((NZ, 2, HALF, FEATS), BF16),
            pltpu.VMEM((NZ, 2, HALF, FEATS), BF16),
            pltpu.VMEM((2, 2, NZ * HALF, FEATS), BF16),
            pltpu.VMEM((NX + 1, D, FEATS), F32),
            pltpu.VMEM((1, FEATS), F32),
            dma((5 + NX,)),
            dma((CHUNKS,)),
            dma((3, CHUNKS)),
            dma((2, CHUNKS)),
            dma((2, CHUNKS)),
            dma((NJ,)),
            dma((NJ,)),
            dma((2, CHUNKS)),
            dma((CHUNKS,)),
            dma((3, NZ)),
            dma((3, NZ)),
        ],
        compiler_params=pltpu.CompilerParams(collective_id=0, has_side_effects=True, vmem_limit_bytes=62 * 2**20),
    )(
        residuals,
        cotangent,
        enc_bias,
        enc_weight,
        jnp.swapaxes(dec_weight, 2, 3),
        active.reshape(CHUNKS, 2, SUB, FEATS),
    )
    dec_grad, enc_grad, bias_grad, feat_grad = pl.pallas_call(
        write_kernel,
        out_shape=tuple(jax.ShapeDtypeStruct(shape, dtype) for shape, dtype in outs),
        in_specs=[vmem] * 4,
        out_specs=(hbm,) * 4,
        scratch_shapes=[dma((4,))],
        compiler_params=pltpu.CompilerParams(vmem_limit_bytes=8 * 2**20),
    )(*held)
    return (
        jnp.swapaxes(dec_grad, 1, 2)[None],
        enc_grad[None],
        bias_grad,
        feat_grad.reshape(1, CHUNKS * TOK, FEATS),
    )


def solution(mesh):
    in_specs = (
        P("layer", "feat", "width"),
        P("layer", "feat", "width"),
        P("layer", "width", "feat"),
        P("layer", "feat"),
        P("layer", None, "feat", "width"),
        P("layer", None, "feat"),
    )
    out_specs = (
        P("layer", None, "feat", "width"),
        P("layer", "width", "feat"),
        P("layer", "feat"),
        P("layer", None, "feat"),
    )
    return jax.shard_map(local, mesh=mesh, in_specs=in_specs, out_specs=out_specs, check_vma=False)
```

```python
import jax
import jax.numpy as jnp
from jax import lax
from jax.experimental import pallas as pl
from jax.experimental.pallas import tpu as pltpu
from jax.sharding import PartitionSpec as P

MESH = pl.DeviceIdType.MESH
BF16, F32 = jnp.bfloat16, jnp.float32

NX, NZ, NJ = 4, 8, 4
TOK = 32
SUB = TOK // 2
HALF = NJ * SUB
D = 576
MAIN = 512
TAIL = D - MAIN
WIDE = 2 * D
FEATS = 256
CHUNKS = NZ * NJ
RING = (1, 2, 3)


def nn(a, b):
    return jnp.dot(a, b, preferred_element_type=F32)


def tn(a, b):
    return lax.dot_general(a, b, (((0,), (0,)), ((), ())), preferred_element_type=F32)


def gather_kernel(
    resid_hbm, cot_hbm, bias_hbm, encw_hbm, decw_hbm, active_hbm,
    dec_out, enc_out, bias_out, fg_out,
    raw, gp, cots, weight, wtail, bias, active,
    part, r1, s2, r2, af,
    loc_sem, p_recv, c_recv, t_recv, z_send, zt_send, y_send, yt_send, x_send,
    r_recv, r_send,
):
    x = lax.axis_index("layer")
    f = lax.axis_index("feat")
    w = lax.axis_index("width")
    z, j = lax.div(f, NJ), lax.rem(f, NJ)
    c = lax.rem(w, 2)

    def at(dx=0, zz=None, jj=None, ww=None):
        zz = z if zz is None else zz
        jj = j if jj is None else jj
        return {"layer": lax.rem(x + dx, NX), "feat": zz * NJ + jj, "width": w if ww is None else ww}

    zi = lambda d: lax.rem(z + d + NZ, NZ)
    hop = (at(zz=zi(1)), at(zz=zi(-1)))
    core_peer = at(ww=w + 1 - 2 * c)
    far_peer = at(ww=lax.rem(w + 2, 4))
    order = [
        j,
        jnp.where(j == 0, 1, j - 1),
        jnp.where(j == 0, 2, jnp.where(j == 3, 1, j + 1)),
        jnp.where(j < 2, 3, 0),
    ]

    slot = lambda d: d + 3
    chunk = lambda d, i: slot(d) * NJ + order[i]

    def when(cond, fn):
        if cond is None:
            fn()
        else:
            pl.when(cond)(fn)

    barrier = pltpu.get_barrier_semaphore()
    peers = [core_peer, far_peer, hop[0], hop[1], at(1), at(2), at(3)] + [at(jj=order[i]) for i in (1, 2, 3)]
    for dev in peers:
        pl.semaphore_signal(barrier, inc=1, device_id=dev, device_id_type=MESH)

    first = [
        pltpu.make_async_copy(resid_hbm.at[0], raw.at[0], loc_sem.at[0]),
        pltpu.make_async_copy(cot_hbm.at[0], raw.at[1], loc_sem.at[1]),
    ]
    for cp in first:
        cp.start()
    loads = [
        (pltpu.make_async_copy(encw_hbm.at[0], weight.at[0], loc_sem.at[2]), None),
        (pltpu.make_async_copy(active_hbm.at[:, c], active, loc_sem.at[3]), None),
        (pltpu.make_async_copy(bias_hbm, bias, loc_sem.at[4]), None),
    ]
    for k in range(NX):
        cp = pltpu.make_async_copy(decw_hbm.at[0, jnp.minimum(x + k, NX - 1)], weight.at[k + 1], loc_sem.at[5 + k])
        loads.append((cp, x + k < NX))
    for cp, cond in loads:
        when(cond, cp.start)

    mine = chunk(0, 0)
    for u in (0, 1):
        first[u].wait()
        rows = raw[u]
        gp[mine, u, :, 0:MAIN] = rows[0:SUB, 0:MAIN]
        gp[mine, u, :, MAIN : 2 * MAIN] = rows[SUB:TOK, 0:MAIN]
        gp[mine, u, :, 2 * MAIN : WIDE] = jnp.concatenate([rows[0:SUB, MAIN:D], rows[SUB:TOK, MAIN:D]], axis=1)
    pl.semaphore_wait(barrier, len(peers))

    def remote(src, dst, ss, rs, dev):
        return pltpu.make_async_remote_copy(src, dst, ss, rs, device_id=dev, device_id_type=MESH)

    def send(cp, cond=None):
        when(cond, cp.start)

    third = x <= 1

    def next_d(r, d):
        return 4 if r == 3 else (r + 1 if d else -r - 1)

    def here(r, d):
        return 4 if r == 4 else (r if d else -r)

    def send_z(r, i, d):
        a, b = chunk(here(r, d), i), chunk(next_d(r, d), i)
        send(remote(gp.at[a], gp.at[b], z_send.at[d], p_recv.at[b], hop[d]))

    def send_zt(r, i, d):
        a, b = chunk(here(r, d), i), chunk(next_d(r, d), i)
        send(remote(cots.at[1, a], cots.at[1, b], zt_send.at[d], t_recv.at[b], hop[d]), third)

    def send_x(a, d, i):
        own, s = gp.at[a, 1], slot(d)
        send(remote(own, cots.at[0, a], x_send.at[0], c_recv.at[0, s], at(3)), x >= 1)
        send(remote(own, cots.at[2, a], x_send.at[1], c_recv.at[1, s], at(1)), x == 3)
        if i not in RING or (d == 0 and i == 0):
            send(remote(own, cots.at[1, a], x_send.at[2], t_recv.at[a], at(2)), x >= 2)

    def wait_p(a):
        remote(gp.at[a], gp.at[a], z_send.at[0], p_recv.at[a], hop[0]).wait_recv()

    def wait_t(a):
        cp = remote(cots.at[1, a], cots.at[1, a], z_send.at[0], t_recv.at[a], hop[0])
        when(third, cp.wait_recv)

    def wait_x(k, d, cond):
        block = cots.at[2 * k, slot(d) * NJ : (slot(d) + 1) * NJ]
        cp = remote(block, block, z_send.at[0], c_recv.at[k, slot(d)], hop[0])
        when(cond, cp.wait_recv)

    def own():
        for d in (0, 1):
            send_z(0, 0, d)
        for i in (1, 2, 3):
            send(remote(gp.at[mine], gp.at[mine], y_send, p_recv.at[mine], at(jj=order[i])))
        send_x(mine, 0, 0)

    to_line = {
        (): (False, False, False),
        (3,): (j == 3, (j == 0) | (j == 3), j == 0),
        (2, 3): (j >= 2, (j == 0) | (j == 3), True),
        (1, 2, 3): (True, True, True),
    }[RING]

    def t0():
        wait_t(mine)
        for i, cond in zip((1, 2, 3), to_line):
            if cond is not False:
                cp = remote(cots.at[1, mine], cots.at[1, mine], yt_send.at[i], t_recv.at[mine], at(jj=order[i]))
                send(cp, third & cond)

    def y(i):
        a = chunk(0, i)
        wait_p(a)
        for d in (0, 1):
            send_z(0, i, d)
        send_x(a, 0, i)

    def ty(i):
        if i in RING:
            wait_t(chunk(0, i))
            for d in (0, 1):
                send_zt(0, i, d)

    def zp(r, i):
        for d in (0, 1):
            if r == 4 and (i < 2) != (d == 0):
                continue
            a = chunk(here(r, d), i)
            wait_p(a)
            if r < 3 or (r == 3 and (i < 2) == (d == 0)):
                send_z(r, i, d)
            send_x(a, here(r, d), i)

    def zt(r, i):
        for d in (0, 1):
            if i not in RING or (r == 4 and (i == 2) != (d == 0)):
                continue
            wait_t(chunk(here(r, d), i))
            if r < 3 or (r == 3 and (i == 2) == (d == 0)):
                send_zt(r, i, d)

    def setup():
        for cp, cond in loads:
            when(cond, cp.wait)
        wtail[...] = jnp.zeros_like(wtail)
        for k in range(NX + 1):
            wtail[k, 0:TAIL, 0:FEATS] = weight[k, MAIN:D, :]
            wtail[k, TAIL : 2 * TAIL, FEATS : 2 * FEATS] = weight[k, MAIN:D, :]
        for t in range(NX):
            @pl.when(t < x)
            def _():
                dec_out[t] = jnp.zeros((D, FEATS), BF16)

    def times(data, k):
        both = jnp.concatenate(
            [data[:, :, 0:MAIN].reshape(HALF, MAIN), data[:, :, MAIN : 2 * MAIN].reshape(HALF, MAIN)], axis=0
        )
        main = nn(both, weight[k, 0:MAIN, :])
        tails = nn(data[:, :, 2 * MAIN :].reshape(HALF, 2 * TAIL), wtail[k])
        return main[0:HALF] + tails[:, 0:FEATS], main[HALF:] + tails[:, FEATS:]

    def pre(d):
        s = slot(d)
        part[0, s, 0], part[0, s, 1] = times(gp[s * NJ : (s + 1) * NJ, 0], 0)
        sum1(0, s).start()

    def act(d):
        wait_x(0, d, x <= 2)
        for i in range(NJ):
            if i not in RING and (d or i):
                wait_t(chunk(d, i))
        wait_x(1, d, x == 0)
        s = slot(d)
        ch = slice(s * NJ, (s + 1) * NJ)
        part[1, s, 0], part[1, s, 1] = times(gp[ch, 1], 1)
        for k, cond in enumerate((x <= 2, x <= 1, x == 0)):
            @pl.when(cond)
            def _():
                a, b = times(cots[k, ch], k + 2)
                part[1, s, 0] += a
                part[1, s, 1] += b
        sum1(1, s).start()

    def sum1(k, s):
        return remote(part.at[k, s, 1 - c], r1.at[k, s], r_send.at[0, k], r_recv.at[0, k, s], core_peer)

    def sum2(k, s):
        return remote(s2.at[k, s], r2.at[k, s], r_send.at[1, k], r_recv.at[1, k, s], far_peer)

    def sum3(k, s, half):
        block = af.at[k, half, s * HALF : (s + 1) * HALF]
        return remote(block, block, r_send.at[2, k], r_recv.at[2, k, s], core_peer)

    def red2(k, d):
        s = slot(d)
        sum1(k, s).wait_recv()
        s2[k, s] = (part[k, s, c] + r1[k, s]).astype(BF16)
        sum2(k, s).start()

    def red3(k, d):
        s = slot(d)
        sum2(k, s).wait_recv()
        total = s2[k, s].astype(F32) + r2[k, s].astype(F32)
        if k == 0:
            total = total + bias[...]
        gate = active[pl.ds(zi(d) * NJ, NJ)].reshape(HALF, FEATS).astype(F32)
        af[k, c, s * HALF : (s + 1) * HALF, :] = (total * gate).astype(BF16)
        sum3(k, s, c).start()

    def red4(k, d):
        s = slot(d)
        sum3(k, s, 1 - c).wait_recv()
        if k == 1:
            for h in (0, 1):
                fg_out[pl.ds(zi(d) * NJ, NJ), h] = af[1, h, s * HALF : (s + 1) * HALF].reshape(NJ, SUB, FEATS)

    def grads(data, k):
        a, b, n = af[k, 0], af[k, 1], NZ * HALF
        main = tn(data[:, :, 0:MAIN].reshape(n, MAIN), a) + tn(data[:, :, MAIN : 2 * MAIN].reshape(n, MAIN), b)
        tails = data[:, :, 2 * MAIN :].reshape(n, 2 * TAIL)
        return main.astype(BF16), (tn(tails, a)[0:TAIL] + tn(tails, b)[TAIL:]).astype(BF16)

    def dec():
        for k in range(NX):
            @pl.when(x + k < NX)
            def _():
                dec_out[x + k, 0:MAIN], dec_out[x + k, MAIN:D] = grads(cots[k - 1] if k else gp[:, 1], 0)

    def enc():
        enc_out[0:MAIN], enc_out[MAIN:D] = grads(gp[:, 0], 1)
        bias_out[...] = sum(jnp.sum(af[1, h].astype(F32), axis=0, keepdims=True) for h in (0, 1))

    def wait_sent():
        def done(ref, sem, cond=None):
            when(cond, remote(ref, ref, sem, p_recv.at[0], hop[0]).wait_send)

        sent = NZ // 2 * NJ - NJ // 2
        for d in (0, 1):
            done(gp.at[0:sent], z_send.at[d])
            n = sum(3 + ((i == 2) == (d == 0)) for i in RING)
            if n:
                done(cots.at[1, 0:n], zt_send.at[d], third)
        done(gp.at[0 : NJ - 1], y_send)
        for i, cond in zip((1, 2, 3), to_line):
            if cond is not False:
                done(cots.at[1, 0], yt_send.at[i], third & cond)
        done(cots.at[0], x_send.at[0], x >= 1)
        done(cots.at[0], x_send.at[1], x == 3)
        direct = CHUNKS - NZ * len(RING)
        done(cots.at[1, 0:direct], x_send.at[2], x >= 2)

    own()
    y(1), zp(1, 0), y(2), zp(1, 1), y(3), t0(), ty(1)
    setup()
    zp(1, 2), ty(2), pre(0), zp(1, 3), ty(3), zp(2, 0), zp(2, 1), act(0), pre(-1)
    zt(1, 1), zt(1, 2), red2(0, 0), pre(1), zp(2, 2), zt(1, 3), act(-1), red2(1, 0), zp(2, 3), red2(0, -1), act(1)
    red2(0, 1), zp(3, 0), zt(2, 1), pre(-2), zt(2, 2), red2(1, -1), pre(2), zp(3, 1), red2(1, 1), zt(2, 3)
    red2(0, -2), act(-2), zp(3, 2), red2(0, 2), act(2), zp(3, 3), red2(1, -2), zt(3, 1), pre(-3), zt(3, 2), red2(1, 2)
    pre(3), red2(0, -3), zt(3, 3), zp(4, 0), zp(4, 2), red2(0, 3), act(-3), zp(4, 1), zp(4, 3), pre(4), red2(1, -3)
    act(3), red2(0, 4), zt(4, 1), zt(4, 2), red2(1, 3), zt(4, 3), act(4)
    for d in (0, -1, 1):
        red3(0, d)
    red2(1, 4)
    for d in (-2, 2, -3, 3):
        red3(0, d)
    for d in (0, -1, 1, -2, 2):
        red3(1, d)
    red3(0, 4)
    wait_sent()
    for d in range(-3, 5):
        red4(0, d)
    dec()
    for d in (-3, 3, 4):
        red3(1, d)
    for d in range(-3, 5):
        red4(1, d)
    enc()
    for k in (0, 1):
        for n, ref in enumerate((r1.at[k], s2.at[k], af.at[k, 0])):
            remote(ref, ref, r_send.at[n, k], p_recv.at[0], hop[0]).wait_send()


def write_kernel(dec, enc, bias, fg, dec_out, enc_out, bias_out, fg_out, sem):
    copies = [
        pltpu.make_async_copy(dec, dec_out, sem.at[0]),
        pltpu.make_async_copy(enc, enc_out, sem.at[1]),
        pltpu.make_async_copy(bias, bias_out, sem.at[2]),
        pltpu.make_async_copy(fg, fg_out, sem.at[3]),
    ]
    for cp in copies:
        cp.start()
    for cp in copies:
        cp.wait()


def local(residuals, cotangent, enc_weight, enc_bias, dec_weight, active):
    vmem, hbm = pl.BlockSpec(memory_space=pltpu.VMEM), pl.BlockSpec(memory_space=pltpu.HBM)
    dma = pltpu.SemaphoreType.DMA
    outs = [((NX, D, FEATS), BF16), ((D, FEATS), BF16), ((1, FEATS), F32), ((CHUNKS, 2, SUB, FEATS), BF16)]
    held = pl.pallas_call(
        gather_kernel,
        out_shape=tuple(pltpu.VMEM(shape, dtype) for shape, dtype in outs),
        in_specs=[hbm] * 6,
        out_specs=(vmem,) * 4,
        scratch_shapes=[
            pltpu.VMEM((2, TOK, D), BF16),
            pltpu.VMEM((CHUNKS, 2, SUB, WIDE), BF16),
            pltpu.VMEM((3, CHUNKS, SUB, WIDE), BF16),
            pltpu.VMEM((NX + 1, D, FEATS), BF16),
            pltpu.VMEM((NX + 1, 2 * TAIL, 2 * FEATS), BF16),
            pltpu.VMEM((1, FEATS), F32),
            pltpu.VMEM((CHUNKS, SUB, FEATS), jnp.int32),
            pltpu.VMEM((2, NZ, 2, HALF, FEATS), F32),
            pltpu.VMEM((2, NZ, HALF, FEATS), F32),
            pltpu.VMEM((2, NZ, HALF, FEATS), BF16),
            pltpu.VMEM((2, NZ, HALF, FEATS), BF16),
            pltpu.VMEM((2, 2, NZ * HALF, FEATS), BF16),
            dma((5 + NX,)),
            dma((CHUNKS,)),
            dma((2, NZ)),
            dma((CHUNKS,)),
            dma((2,)),
            dma((2,)),
            dma,
            dma((NJ,)),
            dma((3,)),
            dma((3, 2, NZ)),
            dma((3, 2)),
        ],
        compiler_params=pltpu.CompilerParams(collective_id=0, has_side_effects=True, vmem_limit_bytes=62 * 2**20),
    )(
        residuals,
        cotangent,
        enc_bias,
        enc_weight,
        jnp.swapaxes(dec_weight, 2, 3),
        active.reshape(CHUNKS, 2, SUB, FEATS),
    )
    dec_grad, enc_grad, bias_grad, feat_grad = pl.pallas_call(
        write_kernel,
        out_shape=tuple(jax.ShapeDtypeStruct(shape, dtype) for shape, dtype in outs),
        in_specs=[vmem] * 4,
        out_specs=(hbm,) * 4,
        scratch_shapes=[dma((4,))],
        compiler_params=pltpu.CompilerParams(vmem_limit_bytes=8 * 2**20),
    )(*held)
    return (
        jnp.swapaxes(dec_grad, 1, 2)[None],
        enc_grad[None],
        bias_grad,
        feat_grad.reshape(1, CHUNKS * TOK, FEATS),
    )


def solution(mesh):
    in_specs = (
        P("layer", "feat", "width"),
        P("layer", "feat", "width"),
        P("layer", "width", "feat"),
        P("layer", "feat"),
        P("layer", None, "feat", "width"),
        P("layer", None, "feat"),
    )
    out_specs = (
        P("layer", None, "feat", "width"),
        P("layer", "width", "feat"),
        P("layer", "feat"),
        P("layer", None, "feat"),
    )
    return jax.shard_map(local, mesh=mesh, in_specs=in_specs, out_specs=out_specs, check_vma=False)
```

```python
import jax
import jax.numpy as jnp
from jax import lax
from jax.experimental import pallas as pl
from jax.experimental.pallas import tpu as pltpu
from jax.sharding import PartitionSpec as P

MESH = pl.DeviceIdType.MESH
BF16, F32 = jnp.bfloat16, jnp.float32

NX, NZ, NJ = 4, 8, 4
TOK = 32
SUB = TOK // 2
HALF = NJ * SUB
D = 576
MAIN = 512
TAIL = D - MAIN
WIDE = 2 * D
FEATS = 256
CHUNKS = NZ * NJ
LAST = NZ - 1
RING = (1, 2, 3)


def nn(a, b):
    return jnp.dot(a, b, preferred_element_type=F32)


def tn(a, b):
    return lax.dot_general(a, b, (((0,), (0,)), ((), ())), preferred_element_type=F32)


def gather_kernel(
    resid_hbm, cot_hbm, bias_hbm, encw_hbm, decw_hbm, active_hbm,
    dec_out, enc_out, bias_out, fg_out,
    raw, gp, cots, weight, wtail, bias, active,
    part, r1, s2, r2, af,
    loc_sem, p_recv, c_recv, t_recv, z_send, zt_send, y_send, yt_send, x_send,
    r_recv, r_send,
):
    x = lax.axis_index("layer")
    f = lax.axis_index("feat")
    w = lax.axis_index("width")
    z, j = lax.div(f, NJ), lax.rem(f, NJ)
    c = lax.rem(w, 2)

    def at(dx=0, zz=None, jj=None, ww=None):
        zz = z if zz is None else zz
        jj = j if jj is None else jj
        return {"layer": lax.rem(x + dx, NX), "feat": zz * NJ + jj, "width": w if ww is None else ww}

    zi = lambda d: lax.rem(z + d + NZ, NZ)
    hop = (at(zz=zi(1)), at(zz=zi(-1)))
    core_peer = at(ww=w + 1 - 2 * c)
    far_peer = at(ww=lax.rem(w + 2, 4))
    order = [
        j,
        jnp.where(j == 0, 1, j - 1),
        jnp.where(j == 0, 2, jnp.where(j == 3, 1, j + 1)),
        jnp.where(j < 2, 3, 0),
    ]

    slot = lambda d: d + 3
    chunk = lambda d, i: slot(d) * NJ + order[i]

    def when(cond, fn):
        if cond is None:
            fn()
        else:
            pl.when(cond)(fn)

    first = [
        pltpu.make_async_copy(resid_hbm.at[0], raw.at[0], loc_sem.at[0]),
        pltpu.make_async_copy(cot_hbm.at[0], raw.at[1], loc_sem.at[1]),
    ]
    for cp in first:
        cp.start()
    barrier = pltpu.get_barrier_semaphore()
    peers = [core_peer, far_peer, hop[0], hop[1], at(1), at(2), at(3)] + [at(jj=order[i]) for i in (1, 2, 3)]
    for dev in peers:
        pl.semaphore_signal(barrier, inc=1, device_id=dev, device_id_type=MESH)

    loads = [
        (pltpu.make_async_copy(encw_hbm.at[0], weight.at[0], loc_sem.at[2]), None),
        (pltpu.make_async_copy(active_hbm.at[:, c], active, loc_sem.at[3]), None),
        (pltpu.make_async_copy(bias_hbm, bias, loc_sem.at[4]), None),
    ]
    for k in range(NX):
        cp = pltpu.make_async_copy(decw_hbm.at[0, jnp.minimum(x + k, NX - 1)], weight.at[k + 1], loc_sem.at[5 + k])
        loads.append((cp, x + k < NX))
    for cp, cond in loads:
        when(cond, cp.start)

    mine = chunk(0, 0)
    for u in (0, 1):
        first[u].wait()
        rows = raw[u]
        gp[mine, u, :, 0:MAIN] = rows[0:SUB, 0:MAIN]
        gp[mine, u, :, MAIN : 2 * MAIN] = rows[SUB:TOK, 0:MAIN]
        gp[mine, u, :, 2 * MAIN : WIDE] = jnp.concatenate([rows[0:SUB, MAIN:D], rows[SUB:TOK, MAIN:D]], axis=1)
    pl.semaphore_wait(barrier, len(peers))

    def remote(src, dst, ss, rs, dev):
        return pltpu.make_async_remote_copy(src, dst, ss, rs, device_id=dev, device_id_type=MESH)

    def send(cp, cond=None):
        when(cond, cp.start)

    third = x <= 1

    def next_d(r, d):
        return 4 if r == 3 else (r + 1 if d else -r - 1)

    def here(r, d):
        return 4 if r == 4 else (r if d else -r)

    def send_z(r, i, d):
        a, b = chunk(here(r, d), i), chunk(next_d(r, d), i)
        send(remote(gp.at[a], gp.at[b], z_send.at[d], p_recv.at[b], hop[d]))

    def send_zt(r, i, d):
        a, b = chunk(here(r, d), i), chunk(next_d(r, d), i)
        send(remote(cots.at[1, a], cots.at[1, b], zt_send.at[d], t_recv.at[b], hop[d]), third)

    straight = lambda d, i: i not in RING or d == 4

    def send_x(a, d, i):
        own, s = gp.at[a, 1], slot(d)
        send(remote(own, cots.at[0, a], x_send.at[0], c_recv.at[0, s], at(3)), x >= 1)
        send(remote(own, cots.at[2, a], x_send.at[1], c_recv.at[1, s], at(1)), x == 3)
        if straight(d, i) or (d == 0 and i == 0):
            send(remote(own, cots.at[1, a], x_send.at[2], t_recv.at[a], at(2)), x >= 2)

    def wait_p(a):
        remote(gp.at[a], gp.at[a], z_send.at[0], p_recv.at[a], hop[0]).wait_recv()

    def wait_t(a):
        cp = remote(cots.at[1, a], cots.at[1, a], z_send.at[0], t_recv.at[a], hop[0])
        when(third, cp.wait_recv)

    def wait_x(k, d, cond):
        block = cots.at[2 * k, slot(d) * NJ : (slot(d) + 1) * NJ]
        cp = remote(block, block, z_send.at[0], c_recv.at[k, slot(d)], hop[0])
        when(cond, cp.wait_recv)

    def own():
        for d in (0, 1):
            send_z(0, 0, d)
        for i in (1, 2, 3):
            send(remote(gp.at[mine], gp.at[mine], y_send, p_recv.at[mine], at(jj=order[i])))
        send_x(mine, 0, 0)

    to_line = {
        (): (False, False, False),
        (3,): (j == 3, (j == 0) | (j == 3), j == 0),
        (2, 3): (j >= 2, (j == 0) | (j == 3), True),
        (1, 2, 3): (True, True, True),
    }[RING]

    def t0():
        wait_t(mine)
        for i, cond in zip((1, 2, 3), to_line):
            if cond is not False:
                cp = remote(cots.at[1, mine], cots.at[1, mine], yt_send.at[i], t_recv.at[mine], at(jj=order[i]))
                send(cp, third & cond)

    def y(i):
        a = chunk(0, i)
        wait_p(a)
        for d in (0, 1):
            send_z(0, i, d)
        send_x(a, 0, i)

    def ty(i):
        if i in RING:
            wait_t(chunk(0, i))
            for d in (0, 1):
                send_zt(0, i, d)

    def zp(r, i):
        for d in (0, 1):
            if r == 4 and (i < 2) != (d == 0):
                continue
            a = chunk(here(r, d), i)
            wait_p(a)
            if r < 3 or (r == 3 and (i < 2) == (d == 0)):
                send_z(r, i, d)
            send_x(a, here(r, d), i)

    def zt(r, i):
        if i in RING:
            for d in (0, 1):
                wait_t(chunk(here(r, d), i))
                if r < 3:
                    send_zt(r, i, d)

    def setup():
        for cp, cond in loads:
            when(cond, cp.wait)
        wtail[...] = jnp.zeros_like(wtail)
        for k in range(NX + 1):
            wtail[k, 0:TAIL, 0:FEATS] = weight[k, MAIN:D, :]
            wtail[k, TAIL : 2 * TAIL, FEATS : 2 * FEATS] = weight[k, MAIN:D, :]
        for t in range(NX):
            @pl.when(t < x)
            def _():
                dec_out[t] = jnp.zeros((D, FEATS), BF16)

    def times(data, k):
        both = jnp.concatenate(
            [data[:, :, 0:MAIN].reshape(HALF, MAIN), data[:, :, MAIN : 2 * MAIN].reshape(HALF, MAIN)], axis=0
        )
        main = nn(both, weight[k, 0:MAIN, :])
        tails = nn(data[:, :, 2 * MAIN :].reshape(HALF, 2 * TAIL), wtail[k])
        return main[0:HALF] + tails[:, 0:FEATS], main[HALF:] + tails[:, FEATS:]

    def pre(d):
        s = slot(d)
        part[0, s, 0], part[0, s, 1] = times(gp[s * NJ : (s + 1) * NJ, 0], 0)
        sum1(0, s).start()

    def act(d):
        wait_x(0, d, x <= 2)
        for i in range(NJ):
            if straight(d, i) and (d or i):
                wait_t(chunk(d, i))
        wait_x(1, d, x == 0)
        s = slot(d)
        ch = slice(s * NJ, (s + 1) * NJ)
        part[1, s, 0], part[1, s, 1] = times(gp[ch, 1], 1)
        for k, cond in enumerate((x <= 2, x <= 1, x == 0)):
            @pl.when(cond)
            def _():
                a, b = times(cots[k, ch], k + 2)
                part[1, s, 0] += a
                part[1, s, 1] += b
        sum1(1, s).start()

    def sum1(k, s):
        return remote(part.at[k, s, 1 - c], r1.at[k, s], r_send.at[0, k], r_recv.at[0, k, s], core_peer)

    def sum2(k, s):
        return remote(s2.at[k, s], r2.at[k, s], r_send.at[1, k], r_recv.at[1, k, s], far_peer)

    def sum3(k, s, half):
        block = af.at[k, half, s * HALF : (s + 1) * HALF]
        return remote(block, block, r_send.at[2, k], r_recv.at[2, k, s], core_peer)

    def red2(k, d):
        s = slot(d)
        sum1(k, s).wait_recv()
        s2[k, s] = (part[k, s, c] + r1[k, s]).astype(BF16)
        sum2(k, s).start()

    def red3(k, d):
        s = slot(d)
        sum2(k, s).wait_recv()
        total = s2[k, s].astype(F32) + r2[k, s].astype(F32)
        if k == 0:
            total = total + bias[...]
        gate = active[pl.ds(zi(d) * NJ, NJ)].reshape(HALF, FEATS).astype(F32)
        af[k, c, s * HALF : (s + 1) * HALF, :] = (total * gate).astype(BF16)
        sum3(k, s, c).start()

    def red4(k, d):
        s = slot(d)
        sum3(k, s, 1 - c).wait_recv()
        if k == 1:
            for h in (0, 1):
                fg_out[pl.ds(zi(d) * NJ, NJ), h] = af[1, h, s * HALF : (s + 1) * HALF].reshape(NJ, SUB, FEATS)

    def grads(data, k):
        a, b, n = af[k, 0], af[k, 1], NZ * HALF
        main = tn(data[:, :, 0:MAIN].reshape(n, MAIN), a) + tn(data[:, :, MAIN : 2 * MAIN].reshape(n, MAIN), b)
        tails = data[:, :, 2 * MAIN :].reshape(n, 2 * TAIL)
        return main.astype(BF16), (tn(tails, a)[0:TAIL] + tn(tails, b)[TAIL:]).astype(BF16)

    def dec():
        for k in range(NX):
            @pl.when(x + k < NX)
            def _():
                dec_out[x + k, 0:MAIN], dec_out[x + k, MAIN:D] = grads(cots[k - 1] if k else gp[:, 1], 0)

    def enc():
        enc_out[0:MAIN], enc_out[MAIN:D] = grads(gp[:, 0], 1)
        bias_out[...] = sum(jnp.sum(af[1, h].astype(F32), axis=0, keepdims=True) for h in (0, 1))

    def wait_sent():
        def done(ref, sem, cond=None):
            when(cond, remote(ref, ref, sem, p_recv.at[0], hop[0]).wait_send)

        sent = NZ // 2 * NJ - NJ // 2
        for d in (0, 1):
            done(gp.at[0:sent], z_send.at[d])
            done(cots.at[1, 0 : 3 * len(RING)], zt_send.at[d], third)
        done(gp.at[0 : NJ - 1], y_send)
        for i, cond in zip((1, 2, 3), to_line):
            if cond is not False:
                done(cots.at[1, 0], yt_send.at[i], third & cond)
        done(cots.at[0], x_send.at[0], x >= 1)
        done(cots.at[0], x_send.at[1], x == 3)
        direct = CHUNKS - LAST * len(RING)
        done(cots.at[1, 0:direct], x_send.at[2], x >= 2)

    own()
    y(1), zp(1, 0), y(2), zp(1, 1), y(3), t0()
    setup()
    zp(1, 2), pre(0), ty(1), zp(1, 3), ty(2), zp(2, 0), ty(3), zp(2, 1), pre(-1), act(0), pre(1)
    zt(1, 1), red2(0, 0), zp(2, 2), zt(1, 2), red2(0, -1), red2(0, 1), zp(2, 3), red2(1, 0), zt(1, 3)
    pre(-2), pre(2), zp(3, 0), act(-1), zt(2, 1), zp(3, 1), act(1), red2(0, -2), zt(2, 2), red2(0, 2), zp(3, 2)
    red2(1, -1), zt(2, 3), red2(1, 1), zp(3, 3), pre(-3), pre(3), act(-2), zt(3, 1), zp(4, 0), zp(4, 2), red2(0, -3)
    act(2), red2(0, 3), zp(4, 1), zp(4, 3), pre(4), red2(1, -2), zt(3, 2), red2(1, 2), zt(3, 3), act(-3)
    red2(0, 4), act(3), red2(1, -3), act(4), red2(1, 3)
    for d in (0, -1, 1, -2, 2):
        red3(0, d)
    red2(1, 4)
    for d in (-3, 3):
        red3(0, d)
    for d in (0, -1, 1, -2, 2):
        red3(1, d)
    red3(0, 4)
    wait_sent()
    for d in range(-3, 5):
        red4(0, d)
    dec()
    for d in (-3, 3, 4):
        red3(1, d)
    for d in range(-3, 5):
        red4(1, d)
    enc()
    for k in (0, 1):
        for n, ref in enumerate((r1.at[k], s2.at[k], af.at[k, 0])):
            remote(ref, ref, r_send.at[n, k], p_recv.at[0], hop[0]).wait_send()


def write_kernel(dec, enc, bias, fg, dec_out, enc_out, bias_out, fg_out, sem):
    copies = [
        pltpu.make_async_copy(dec, dec_out, sem.at[0]),
        pltpu.make_async_copy(enc, enc_out, sem.at[1]),
        pltpu.make_async_copy(bias, bias_out, sem.at[2]),
        pltpu.make_async_copy(fg, fg_out, sem.at[3]),
    ]
    for cp in copies:
        cp.start()
    for cp in copies:
        cp.wait()


def local(residuals, cotangent, enc_weight, enc_bias, dec_weight, active):
    vmem, hbm = pl.BlockSpec(memory_space=pltpu.VMEM), pl.BlockSpec(memory_space=pltpu.HBM)
    dma = pltpu.SemaphoreType.DMA
    outs = [((NX, D, FEATS), BF16), ((D, FEATS), BF16), ((1, FEATS), F32), ((CHUNKS, 2, SUB, FEATS), BF16)]
    held = pl.pallas_call(
        gather_kernel,
        out_shape=tuple(pltpu.VMEM(shape, dtype) for shape, dtype in outs),
        in_specs=[hbm] * 6,
        out_specs=(vmem,) * 4,
        scratch_shapes=[
            pltpu.VMEM((2, TOK, D), BF16),
            pltpu.VMEM((CHUNKS, 2, SUB, WIDE), BF16),
            pltpu.VMEM((3, CHUNKS, SUB, WIDE), BF16),
            pltpu.VMEM((NX + 1, D, FEATS), BF16),
            pltpu.VMEM((NX + 1, 2 * TAIL, 2 * FEATS), BF16),
            pltpu.VMEM((1, FEATS), F32),
            pltpu.VMEM((CHUNKS, SUB, FEATS), jnp.int32),
            pltpu.VMEM((2, NZ, 2, HALF, FEATS), F32),
            pltpu.VMEM((2, NZ, HALF, FEATS), F32),
            pltpu.VMEM((2, NZ, HALF, FEATS), BF16),
            pltpu.VMEM((2, NZ, HALF, FEATS), BF16),
            pltpu.VMEM((2, 2, NZ * HALF, FEATS), BF16),
            dma((5 + NX,)),
            dma((CHUNKS,)),
            dma((2, NZ)),
            dma((CHUNKS,)),
            dma((2,)),
            dma((2,)),
            dma,
            dma((NJ,)),
            dma((3,)),
            dma((3, 2, NZ)),
            dma((3, 2)),
        ],
        compiler_params=pltpu.CompilerParams(collective_id=0, has_side_effects=True, vmem_limit_bytes=62 * 2**20),
    )(
        residuals,
        cotangent,
        enc_bias,
        enc_weight,
        jnp.swapaxes(dec_weight, 2, 3),
        active.reshape(CHUNKS, 2, SUB, FEATS),
    )
    dec_grad, enc_grad, bias_grad, feat_grad = pl.pallas_call(
        write_kernel,
        out_shape=tuple(jax.ShapeDtypeStruct(shape, dtype) for shape, dtype in outs),
        in_specs=[vmem] * 4,
        out_specs=(hbm,) * 4,
        scratch_shapes=[dma((4,))],
        compiler_params=pltpu.CompilerParams(vmem_limit_bytes=8 * 2**20),
    )(*held)
    return (
        jnp.swapaxes(dec_grad, 1, 2)[None],
        enc_grad[None],
        bias_grad,
        feat_grad.reshape(1, CHUNKS * TOK, FEATS),
    )


def solution(mesh):
    in_specs = (
        P("layer", "feat", "width"),
        P("layer", "feat", "width"),
        P("layer", "width", "feat"),
        P("layer", "feat"),
        P("layer", None, "feat", "width"),
        P("layer", None, "feat"),
    )
    out_specs = (
        P("layer", None, "feat", "width"),
        P("layer", "width", "feat"),
        P("layer", "feat"),
        P("layer", None, "feat"),
    )
    return jax.shard_map(local, mesh=mesh, in_specs=in_specs, out_specs=out_specs, check_vma=False)
```

```python
import jax
import jax.numpy as jnp
from jax import lax
from jax.experimental import pallas as pl
from jax.experimental.pallas import tpu as pltpu
from jax.sharding import PartitionSpec as P

MESH = pl.DeviceIdType.MESH
BF16, F32 = jnp.bfloat16, jnp.float32

NX, NZ, NJ = 4, 8, 4
TOK = 32
SUB = TOK // 2
HALF = NJ * SUB
D = 576
MAIN = 512
TAIL = D - MAIN
WIDE = 2 * D
FEATS = 256
CHUNKS = NZ * NJ
LAST = NZ - 1
RING = (1, 2, 3)


def nn(a, b):
    return jnp.dot(a, b, preferred_element_type=F32)


def tn(a, b):
    return lax.dot_general(a, b, (((0,), (0,)), ((), ())), preferred_element_type=F32)


def gather_kernel(
    resid_hbm, cot_hbm, bias_hbm, encw_hbm, decw_hbm, active_hbm,
    dec_out, enc_out, bias_out, fg_out,
    raw, gp, cots, weight, wtail, bias, active,
    part, r1, s2, r2, af,
    loc_sem, p_recv, c_recv, t_recv, z_send, zt_send, y_send, yt_send, x_send,
    r_recv, r_send,
):
    x = lax.axis_index("layer")
    f = lax.axis_index("feat")
    w = lax.axis_index("width")
    z, j = lax.div(f, NJ), lax.rem(f, NJ)
    c = lax.rem(w, 2)

    def at(dx=0, zz=None, jj=None, ww=None):
        zz = z if zz is None else zz
        jj = j if jj is None else jj
        return {"layer": lax.rem(x + dx, NX), "feat": zz * NJ + jj, "width": w if ww is None else ww}

    zi = lambda d: lax.rem(z + d + NZ, NZ)
    hop = (at(zz=zi(1)), at(zz=zi(-1)))
    core_peer = at(ww=w + 1 - 2 * c)
    far_peer = at(ww=lax.rem(w + 2, 4))
    order = [
        j,
        jnp.where(j == 0, 1, j - 1),
        jnp.where(j == 0, 2, jnp.where(j == 3, 1, j + 1)),
        jnp.where(j < 2, 3, 0),
    ]

    slot = lambda d: d + 3
    chunk = lambda d, i: slot(d) * NJ + order[i]

    def when(cond, fn):
        if cond is None:
            fn()
        else:
            pl.when(cond)(fn)

    first = [
        pltpu.make_async_copy(resid_hbm.at[0], raw.at[0], loc_sem.at[0]),
        pltpu.make_async_copy(cot_hbm.at[0], raw.at[1], loc_sem.at[1]),
    ]
    for cp in first:
        cp.start()
    barrier = pltpu.get_barrier_semaphore()
    peers = [core_peer, far_peer, hop[0], hop[1], at(1), at(2), at(3)] + [at(jj=order[i]) for i in (1, 2, 3)]
    for dev in peers:
        pl.semaphore_signal(barrier, inc=1, device_id=dev, device_id_type=MESH)

    loads = [
        (pltpu.make_async_copy(encw_hbm.at[0], weight.at[0], loc_sem.at[2]), None),
        (pltpu.make_async_copy(active_hbm.at[:, c], active, loc_sem.at[3]), None),
        (pltpu.make_async_copy(bias_hbm, bias, loc_sem.at[4]), None),
    ]
    for k in range(NX):
        cp = pltpu.make_async_copy(decw_hbm.at[0, jnp.minimum(x + k, NX - 1)], weight.at[k + 1], loc_sem.at[5 + k])
        loads.append((cp, x + k < NX))
    for cp, cond in loads:
        when(cond, cp.start)

    mine = chunk(0, 0)
    for u in (0, 1):
        first[u].wait()
        rows = raw[u]
        gp[mine, u, :, 0:MAIN] = rows[0:SUB, 0:MAIN]
        gp[mine, u, :, MAIN : 2 * MAIN] = rows[SUB:TOK, 0:MAIN]
        gp[mine, u, :, 2 * MAIN : WIDE] = jnp.concatenate([rows[0:SUB, MAIN:D], rows[SUB:TOK, MAIN:D]], axis=1)
    pl.semaphore_wait(barrier, len(peers))

    def remote(src, dst, ss, rs, dev):
        return pltpu.make_async_remote_copy(src, dst, ss, rs, device_id=dev, device_id_type=MESH)

    def send(cp, cond=None):
        when(cond, cp.start)

    third = x <= 1

    def next_d(r, d):
        return 4 if r == 3 else (r + 1 if d else -r - 1)

    def here(r, d):
        return 4 if r == 4 else (r if d else -r)

    def send_z(r, i, d):
        a, b = chunk(here(r, d), i), chunk(next_d(r, d), i)
        send(remote(gp.at[a], gp.at[b], z_send.at[d], p_recv.at[b], hop[d]))

    def send_zt(r, i, d):
        a, b = chunk(here(r, d), i), chunk(next_d(r, d), i)
        send(remote(cots.at[1, a], cots.at[1, b], zt_send.at[d], t_recv.at[b], hop[d]), third)

    straight = lambda d, i: i not in RING or d == 4

    def send_x(a, d, i):
        own, s = gp.at[a, 1], slot(d)
        send(remote(own, cots.at[0, a], x_send.at[0], c_recv.at[0, s], at(3)), x >= 1)
        send(remote(own, cots.at[2, a], x_send.at[1], c_recv.at[1, s], at(1)), x == 3)
        if straight(d, i) or (d == 0 and i == 0):
            send(remote(own, cots.at[1, a], x_send.at[2], t_recv.at[a], at(2)), x >= 2)

    def wait_p(a):
        remote(gp.at[a], gp.at[a], z_send.at[0], p_recv.at[a], hop[0]).wait_recv()

    def wait_t(a):
        cp = remote(cots.at[1, a], cots.at[1, a], z_send.at[0], t_recv.at[a], hop[0])
        when(third, cp.wait_recv)

    def wait_x(k, d, cond):
        block = cots.at[2 * k, slot(d) * NJ : (slot(d) + 1) * NJ]
        cp = remote(block, block, z_send.at[0], c_recv.at[k, slot(d)], hop[0])
        when(cond, cp.wait_recv)

    def own():
        for d in (0, 1):
            send_z(0, 0, d)
        for i in (1, 2, 3):
            send(remote(gp.at[mine], gp.at[mine], y_send, p_recv.at[mine], at(jj=order[i])))
        send_x(mine, 0, 0)

    to_line = {
        (): (False, False, False),
        (3,): (j == 3, (j == 0) | (j == 3), j == 0),
        (2, 3): (j >= 2, (j == 0) | (j == 3), True),
        (1, 2, 3): (True, True, True),
    }[RING]

    def t0():
        wait_t(mine)
        for i, cond in zip((1, 2, 3), to_line):
            if cond is not False:
                cp = remote(cots.at[1, mine], cots.at[1, mine], yt_send.at[i], t_recv.at[mine], at(jj=order[i]))
                send(cp, third & cond)

    def y(i):
        a = chunk(0, i)
        wait_p(a)
        for d in (0, 1):
            send_z(0, i, d)
        send_x(a, 0, i)

    def ty(i):
        if i in RING:
            wait_t(chunk(0, i))
            for d in (0, 1):
                send_zt(0, i, d)

    def zp(r, i):
        for d in (0, 1):
            if r == 4 and (i < 2) != (d == 0):
                continue
            a = chunk(here(r, d), i)
            wait_p(a)
            if r < 3 or (r == 3 and (i < 2) == (d == 0)):
                send_z(r, i, d)
            send_x(a, here(r, d), i)

    def zt(r, i):
        if i in RING:
            for d in (0, 1):
                wait_t(chunk(here(r, d), i))
                if r < 3:
                    send_zt(r, i, d)

    def setup():
        for cp, cond in loads:
            when(cond, cp.wait)
        wtail[...] = jnp.zeros_like(wtail)
        for k in range(NX + 1):
            wtail[k, 0:TAIL, 0:FEATS] = weight[k, MAIN:D, :]
            wtail[k, TAIL : 2 * TAIL, FEATS : 2 * FEATS] = weight[k, MAIN:D, :]
        for t in range(NX):
            @pl.when(t < x)
            def _():
                dec_out[t] = jnp.zeros((D, FEATS), BF16)

    def times(data, k):
        both = jnp.concatenate(
            [data[:, :, 0:MAIN].reshape(HALF, MAIN), data[:, :, MAIN : 2 * MAIN].reshape(HALF, MAIN)], axis=0
        )
        main = nn(both, weight[k, 0:MAIN, :])
        tails = nn(data[:, :, 2 * MAIN :].reshape(HALF, 2 * TAIL), wtail[k])
        return main[0:HALF] + tails[:, 0:FEATS], main[HALF:] + tails[:, FEATS:]

    def pre(d):
        s = slot(d)
        part[0, s, 0], part[0, s, 1] = times(gp[s * NJ : (s + 1) * NJ, 0], 0)
        sum1(0, s).start()

    def act(d):
        wait_x(0, d, x <= 2)
        for i in range(NJ):
            if straight(d, i) and (d or i):
                wait_t(chunk(d, i))
        wait_x(1, d, x == 0)
        s = slot(d)
        ch = slice(s * NJ, (s + 1) * NJ)
        part[1, s, 0], part[1, s, 1] = times(gp[ch, 1], 1)
        for k, cond in enumerate((x <= 2, x <= 1, x == 0)):
            @pl.when(cond)
            def _():
                a, b = times(cots[k, ch], k + 2)
                part[1, s, 0] += a
                part[1, s, 1] += b
        sum1(1, s).start()

    def sum1(k, s):
        return remote(part.at[k, s, 1 - c], r1.at[k, s], r_send.at[0, k], r_recv.at[0, k, s], core_peer)

    def sum2(k, s):
        return remote(s2.at[k, s], r2.at[k, s], r_send.at[1, k], r_recv.at[1, k, s], far_peer)

    def sum3(k, s, half):
        block = af.at[k, half, s * HALF : (s + 1) * HALF]
        return remote(block, block, r_send.at[2, k], r_recv.at[2, k, s], core_peer)

    def red2(k, d):
        s = slot(d)
        sum1(k, s).wait_recv()
        s2[k, s] = (part[k, s, c] + r1[k, s]).astype(BF16)
        sum2(k, s).start()

    def red3(k, d):
        s = slot(d)
        sum2(k, s).wait_recv()
        total = s2[k, s].astype(F32) + r2[k, s].astype(F32)
        if k == 0:
            total = total + bias[...]
        gate = active[pl.ds(zi(d) * NJ, NJ)].reshape(HALF, FEATS).astype(F32)
        done = (total * gate).astype(BF16)
        af[k, c, s * HALF : (s + 1) * HALF, :] = done
        sum3(k, s, c).start()
        if k == 1:
            fg_out[pl.ds(zi(d) * NJ, NJ), c] = done.reshape(NJ, SUB, FEATS)

    def red4(k, d):
        s = slot(d)
        sum3(k, s, 1 - c).wait_recv()
        if k == 1:
            fg_out[pl.ds(zi(d) * NJ, NJ), 1 - c] = af[1, 1 - c, s * HALF : (s + 1) * HALF].reshape(NJ, SUB, FEATS)

    def grads(data, k):
        a, b, n = af[k, 0], af[k, 1], NZ * HALF
        main = tn(data[:, :, 0:MAIN].reshape(n, MAIN), a) + tn(data[:, :, MAIN : 2 * MAIN].reshape(n, MAIN), b)
        tails = data[:, :, 2 * MAIN :].reshape(n, 2 * TAIL)
        return main.astype(BF16), (tn(tails, a)[0:TAIL] + tn(tails, b)[TAIL:]).astype(BF16)

    def dec():
        for k in range(NX):
            @pl.when(x + k < NX)
            def _():
                dec_out[x + k, 0:MAIN], dec_out[x + k, MAIN:D] = grads(cots[k - 1] if k else gp[:, 1], 0)

    def enc():
        enc_out[0:MAIN], enc_out[MAIN:D] = grads(gp[:, 0], 1)
        bias_out[...] = sum(jnp.sum(af[1, h].astype(F32), axis=0, keepdims=True) for h in (0, 1))

    def wait_sent():
        def done(ref, sem, cond=None):
            when(cond, remote(ref, ref, sem, p_recv.at[0], hop[0]).wait_send)

        sent = NZ // 2 * NJ - NJ // 2
        for d in (0, 1):
            done(gp.at[0:sent], z_send.at[d])
            done(cots.at[1, 0 : 3 * len(RING)], zt_send.at[d], third)
        done(gp.at[0 : NJ - 1], y_send)
        for i, cond in zip((1, 2, 3), to_line):
            if cond is not False:
                done(cots.at[1, 0], yt_send.at[i], third & cond)
        done(cots.at[0], x_send.at[0], x >= 1)
        done(cots.at[0], x_send.at[1], x == 3)
        direct = CHUNKS - LAST * len(RING)
        done(cots.at[1, 0:direct], x_send.at[2], x >= 2)

    own()
    y(1), zp(1, 0), y(2), zp(1, 1), y(3), t0()
    setup()
    zp(1, 2), pre(0), ty(1), zp(1, 3), ty(2), zp(2, 0), ty(3), zp(2, 1), pre(-1), act(0), pre(1)
    zt(1, 1), red2(0, 0), zp(2, 2), zt(1, 2), red2(0, -1), red2(0, 1), zp(2, 3), red2(1, 0), zt(1, 3)
    pre(-2), pre(2), zp(3, 0), act(-1), zt(2, 1), zp(3, 1), act(1), red2(0, -2), zt(2, 2), red2(0, 2), zp(3, 2)
    red2(1, -1), zt(2, 3), red2(1, 1), zp(3, 3), pre(-3), pre(3), act(-2), zt(3, 1), zp(4, 0), zp(4, 2), red2(0, -3)
    act(2), red2(0, 3), zp(4, 1), zp(4, 3), pre(4), red2(1, -2), zt(3, 2), red2(1, 2), zt(3, 3), red2(0, 4)
    act(-3), act(3), red2(1, -3), act(4), red2(1, 3)
    for d in (0, -1, 1, -2, 2):
        red3(0, d)
    red2(1, 4)
    for d in (-3, 3):
        red3(0, d)
    for d in (0, -1, 1, -2, 2):
        red3(1, d)
    red3(0, 4)
    wait_sent()
    for d in range(-3, 5):
        red4(0, d)
    dec()
    for d in (-3, 3, 4):
        red3(1, d)
    for d in range(-3, 5):
        red4(1, d)
    enc()
    for k in (0, 1):
        for n, ref in enumerate((r1.at[k], s2.at[k], af.at[k, 0])):
            remote(ref, ref, r_send.at[n, k], p_recv.at[0], hop[0]).wait_send()


def write_kernel(dec, enc, bias, fg, dec_out, enc_out, bias_out, fg_out, sem):
    copies = [
        pltpu.make_async_copy(dec, dec_out, sem.at[0]),
        pltpu.make_async_copy(enc, enc_out, sem.at[1]),
        pltpu.make_async_copy(bias, bias_out, sem.at[2]),
        pltpu.make_async_copy(fg, fg_out, sem.at[3]),
    ]
    for cp in copies:
        cp.start()
    for cp in copies:
        cp.wait()


def local(residuals, cotangent, enc_weight, enc_bias, dec_weight, active):
    vmem, hbm = pl.BlockSpec(memory_space=pltpu.VMEM), pl.BlockSpec(memory_space=pltpu.HBM)
    dma = pltpu.SemaphoreType.DMA
    outs = [((NX, D, FEATS), BF16), ((D, FEATS), BF16), ((1, FEATS), F32), ((CHUNKS, 2, SUB, FEATS), BF16)]
    held = pl.pallas_call(
        gather_kernel,
        out_shape=tuple(pltpu.VMEM(shape, dtype) for shape, dtype in outs),
        in_specs=[hbm] * 6,
        out_specs=(vmem,) * 4,
        scratch_shapes=[
            pltpu.VMEM((2, TOK, D), BF16),
            pltpu.VMEM((CHUNKS, 2, SUB, WIDE), BF16),
            pltpu.VMEM((3, CHUNKS, SUB, WIDE), BF16),
            pltpu.VMEM((NX + 1, D, FEATS), BF16),
            pltpu.VMEM((NX + 1, 2 * TAIL, 2 * FEATS), BF16),
            pltpu.VMEM((1, FEATS), F32),
            pltpu.VMEM((CHUNKS, SUB, FEATS), jnp.int32),
            pltpu.VMEM((2, NZ, 2, HALF, FEATS), F32),
            pltpu.VMEM((2, NZ, HALF, FEATS), F32),
            pltpu.VMEM((2, NZ, HALF, FEATS), BF16),
            pltpu.VMEM((2, NZ, HALF, FEATS), BF16),
            pltpu.VMEM((2, 2, NZ * HALF, FEATS), BF16),
            dma((5 + NX,)),
            dma((CHUNKS,)),
            dma((2, NZ)),
            dma((CHUNKS,)),
            dma((2,)),
            dma((2,)),
            dma,
            dma((NJ,)),
            dma((3,)),
            dma((3, 2, NZ)),
            dma((3, 2)),
        ],
        compiler_params=pltpu.CompilerParams(collective_id=0, has_side_effects=True, vmem_limit_bytes=62 * 2**20),
    )(
        residuals,
        cotangent,
        enc_bias,
        enc_weight,
        jnp.swapaxes(dec_weight, 2, 3),
        active.reshape(CHUNKS, 2, SUB, FEATS),
    )
    dec_grad, enc_grad, bias_grad, feat_grad = pl.pallas_call(
        write_kernel,
        out_shape=tuple(jax.ShapeDtypeStruct(shape, dtype) for shape, dtype in outs),
        in_specs=[vmem] * 4,
        out_specs=(hbm,) * 4,
        scratch_shapes=[dma((4,))],
        compiler_params=pltpu.CompilerParams(vmem_limit_bytes=8 * 2**20),
    )(*held)
    return (
        jnp.swapaxes(dec_grad, 1, 2)[None],
        enc_grad[None],
        bias_grad,
        feat_grad.reshape(1, CHUNKS * TOK, FEATS),
    )


def solution(mesh):
    in_specs = (
        P("layer", "feat", "width"),
        P("layer", "feat", "width"),
        P("layer", "width", "feat"),
        P("layer", "feat"),
        P("layer", None, "feat", "width"),
        P("layer", None, "feat"),
    )
    out_specs = (
        P("layer", None, "feat", "width"),
        P("layer", "width", "feat"),
        P("layer", "feat"),
        P("layer", None, "feat"),
    )
    return jax.shard_map(local, mesh=mesh, in_specs=in_specs, out_specs=out_specs, check_vma=False)
```
